768 devices in a mesh: slab: 64 (over y, x, core), sub: 12 (over z).
Axes of the slice: x: 4, y: 8, z: 12, core: 2. Of those that a mesh axis runs over, the one named last changes fastest.
Arguments:
- field_init: float32 [3, 512, 192, 128], P(None, 'slab', 'sub'), may hold values from -6 to 6
- load: float32 [3, 512, 192, 128], P(None, 'slab', 'sub'), may hold values from -6 to 6
- modulus: float32 [512, 192, 128], P('slab', 'sub'), may hold values from 0.3 to 3
- seg_z: int32 [512], P('slab'), may hold values from 0 to 127, as said below
- seg_y: int32 [192], P('sub'), may hold values from 0 to 47, as said below
- seg_x: int32 [128], replicated, may hold values from 0 to 31, as said below
Outputs:
- smoothed: float32 [3, 512, 192, 128], P(None, 'slab', 'sub')
- coarse: float32 [6, 128, 1536], P(None, 'slab', 'sub')
The draws below stay inside these ranges and needn't reach their ends.
Inputs may be any that keep to these rules, and one draw needn't show every extreme that they name: `seg_z`: along z, segment k starts at node 4 k or 4 k + 1 (segment 0 at 0, the last segment at 4 k + 1) and runs to the next start or the grid's end; entries never fall. `seg_y`: along y, segment k starts at node 4 k or 4 k + 1 (segment 0 at 0, the last segment at 4 k + 1) and runs to the next start or the grid's end; entries never fall. `seg_x`: along x, segment k starts at node 4 k or 4 k + 1 (segment 0 at 0, the last segment at 4 k + 1) and runs to the next start or the grid's end; entries never fall.
All inputs are finite; a program needn't handle non-finite values.
Results may differ from the reference program's by a relative error of at most 0.0003.
Values sent between devices are 32-bit elements; how exact they have to be, the bound alone decides.
No kernel may reach another device: no remote copies, remote signals or barrier semaphores. Data moves between devices by JAX's collectives and lax.ppermute only.
A program may use at most 32 MiB of HBM per device.

```python
import math
import jax
import jax.numpy as jnp
import numpy as np
from jax import lax

CX = 128
CZ = 8
SWEEPS = 2
SX = 32
NY = 192
NZ = 512
NSY = 48
NSZ = 128
N_SLAB = 64


def segment_index(key, extent, pieces):
    jitter = jax.random.randint(key, (pieces,), 0, 2).astype(jnp.int32)
    order = jnp.arange(pieces, dtype=jnp.int32)
    jitter = jitter * (order > 0).astype(jnp.int32)
    jitter = jnp.where(order == pieces - 1, jnp.int32(1), jitter).astype(jnp.int32)
    starts = 4 * order + jitter
    places = jnp.arange(extent, dtype=jnp.int32)
    return (jnp.sum((places[:, None] >= starts[None, :]).astype(jnp.int32), axis=1) - 1).astype(jnp.int32)


def draw_seg_z(key, part):
    return segment_index(jax.random.fold_in(key, 11), NZ, NSZ)


def draw_seg_y(key, part):
    return segment_index(jax.random.fold_in(key, 23), NY, NSY)


def draw_seg_x(key, part):
    return segment_index(jax.random.fold_in(key, 37), CX, SX)


def block_levels(stream_key, dims, cuts, smallest, largest):
    def one(axis_at, blocks):
        draws = jax.random.uniform(jax.random.fold_in(jax.random.fold_in(stream_key, 6), axis_at), (blocks,), jnp.float32, smallest / len(cuts), largest / len(cuts))
        return jnp.repeat(jnp.exp(draws), dims[axis_at] // blocks).reshape((-1,) + (1,) * (len(dims) - axis_at - 1))

    factor_of = one(*cuts[0])
    for cut in cuts[1:]:
        factor_of = factor_of * one(*cut)
    return factor_of


def normal_values(key, shape, width, limit, cuts=(), kind=jnp.bfloat16):
    values = jax.random.normal(key, shape, jnp.float32) * width
    if len(cuts) > 0:
        values = block_levels(key, shape, cuts, -0.22, 0.18) * values
    return jnp.clip(values, min=-limit, max=limit).astype(kind)


def setup_inputs(seed: int = 0) -> dict:
    arg_keys = jax.random.split(jax.random.key(seed), 7)
    field_init = normal_values(arg_keys[0], (3, NZ, NY, CX), 1.0, 6.0, ((1, 64), (2, 12)), jnp.float32)
    load = normal_values(arg_keys[1], (3, NZ, NY, CX), 1.0, 6.0, ((1, 64), (2, 12)), jnp.float32)
    modulus = jnp.clip(jnp.exp(math.log(3.0) - 2.3025851 * jax.random.uniform(arg_keys[2], (NZ, NY, CX), jnp.float32) ** block_levels(arg_keys[2], (NZ, NY, CX), ((0, 64), (1, 12)), -0.2, 0.2)), 0.3, 3.0)
    seg_z = draw_seg_z(jax.random.fold_in(arg_keys[6], 71), 0)
    seg_y = draw_seg_y(jax.random.fold_in(arg_keys[6], 71), 0)
    seg_x = draw_seg_x(jax.random.fold_in(arg_keys[6], 71), 0)
    return dict(field_init=field_init, load=load, modulus=modulus, seg_z=seg_z, seg_y=seg_y, seg_x=seg_x)


damping = 0.6

def hex_stiffness():
    poisson = 0.3
    lame_first = poisson / ((1.0 + poisson) * (1.0 - 2.0 * poisson))
    lame_shear = 0.5 / (1.0 + poisson)
    elastic = np.zeros((6, 6))
    elastic[:3, :3] = lame_first
    for entry in range(3):
        elastic[entry, entry] += 2.0 * lame_shear
        elastic[entry + 3, entry + 3] = lame_shear
    points = [0.5 - 0.5 / np.sqrt(3.0), 0.5 + 0.5 / np.sqrt(3.0)]
    stiffness = np.zeros((24, 24))
    for point_z in points:
        for point_y in points:
            for point_x in points:
                strain = np.zeros((6, 24))
                for corner in range(8):
                    corner_z, corner_y, corner_x = (corner // 4, corner // 2 % 2, corner % 2)
                    shape_x = point_x if corner_x else 1.0 - point_x
                    shape_y = point_y if corner_y else 1.0 - point_y
                    shape_z = point_z if corner_z else 1.0 - point_z
                    slope_x = (1.0 if corner_x else -1.0) * shape_y * shape_z
                    slope_y = (1.0 if corner_y else -1.0) * shape_x * shape_z
                    slope_z = (1.0 if corner_z else -1.0) * shape_x * shape_y
                    column = 3 * corner
                    strain[0, column] = slope_x
                    strain[1, column + 1] = slope_y
                    strain[2, column + 2] = slope_z
                    strain[3, column] = slope_y
                    strain[3, column + 1] = slope_x
                    strain[4, column + 1] = slope_z
                    strain[4, column + 2] = slope_y
                    strain[5, column] = slope_z
                    strain[5, column + 2] = slope_x
                stiffness += strain.T @ elastic @ strain / 8.0
    return stiffness

def shift_right(values):
    return jnp.concatenate([jnp.zeros_like(values[..., :1]), values[..., :-1]], axis=-1)

def shift_left(values):
    return jnp.concatenate([values[..., 1:], jnp.zeros_like(values[..., :1])], axis=-1)

def apply_op(field_ext, mod_ext, table):
    depth = field_ext.shape[1] - 2
    rows = field_ext.shape[2] - 2
    element = mod_ext[:depth + 1, :rows + 1, :]
    corners = []
    for corner in range(8):
        corner_z, corner_y, corner_x = (corner // 4, corner // 2 % 2, corner % 2)
        piece = field_ext[:, corner_z:corner_z + depth + 1, corner_y:corner_y + rows + 1, :]
        if corner_x:
            piece = shift_left(piece)
        corners.append(piece)
    stacked = jnp.concatenate(corners, axis=0)
    forces = jnp.einsum('ij,jzyx->izyx', table, stacked, precision=lax.Precision.HIGHEST) * element[None]
    result = jnp.zeros((3, depth, rows, field_ext.shape[3]), jnp.float32)
    for corner in range(8):
        corner_z, corner_y, corner_x = (corner // 4, corner // 2 % 2, corner % 2)
        piece = forces[3 * corner:3 * corner + 3, 1 - corner_z:1 - corner_z + depth, 1 - corner_y:1 - corner_y + rows, :]
        if corner_x:
            piece = shift_right(piece)
        result = result + piece
    return result

def inverse_blocks(mod_ext, outside, table):
    depth = mod_ext.shape[0] - 2
    rows = mod_ext.shape[1] - 2
    diagonal = jnp.zeros((3, 3, depth, rows, mod_ext.shape[2]), jnp.float32)
    for corner in range(8):
        corner_z, corner_y, corner_x = (corner // 4, corner // 2 % 2, corner % 2)
        piece = mod_ext[1 - corner_z:1 - corner_z + depth, 1 - corner_y:1 - corner_y + rows, :]
        if corner_x:
            piece = shift_right(piece)
        block = table[3 * corner:3 * corner + 3, 3 * corner:3 * corner + 3]
        diagonal = diagonal + block[:, :, None, None, None] * piece[None, None]
    diagonal = diagonal + jnp.eye(3, dtype=jnp.float32)[:, :, None, None, None] * outside[None, None]
    a00, a01, a02 = (diagonal[0, 0], diagonal[0, 1], diagonal[0, 2])
    a10, a11, a12 = (diagonal[1, 0], diagonal[1, 1], diagonal[1, 2])
    a20, a21, a22 = (diagonal[2, 0], diagonal[2, 1], diagonal[2, 2])
    co00 = a11 * a22 - a12 * a21
    co01 = a12 * a20 - a10 * a22
    co02 = a10 * a21 - a11 * a20
    determinant = a00 * co00 + a01 * co01 + a02 * co02
    rows_inv = [[co00, a02 * a21 - a01 * a22, a01 * a12 - a02 * a11], [co01, a00 * a22 - a02 * a20, a02 * a10 - a00 * a12], [co02, a01 * a20 - a00 * a21, a00 * a11 - a01 * a10]]
    return jnp.stack([jnp.stack(line, axis=0) for line in rows_inv], axis=0) / determinant[None, None]

def block_mult(inverse, vector):
    return lax.optimization_barrier(jnp.sum(inverse * vector[None], axis=1))

def cross(first, second):
    return (first[1] * second[2] - first[2] * second[1], first[2] * second[0] - first[0] * second[2], first[0] * second[1] - first[1] * second[0])

def node_terms(residual, offset_x, offset_y, offset_z):
    shape = residual.shape[1:]
    offsets = [jnp.broadcast_to(offset_x, shape), jnp.broadcast_to(offset_y, shape), jnp.broadcast_to(offset_z, shape)]
    turned = cross(offsets, [residual[0], residual[1], residual[2]])
    return [residual[0], residual[1], residual[2], turned[0], turned[1], turned[2], offsets[0], offsets[1], offsets[2], jnp.ones(shape, jnp.float32)]

def finalize(sums):
    count = sums[9]
    norm_root = jnp.sqrt(count)
    centre = [sums[6] / count, sums[7] / count, sums[8] / count]
    moved = [sums[0], sums[1], sums[2]]
    turned = cross(centre, moved)
    rotation = [sums[3 + k] - turned[k] for k in range(3)]
    return jnp.stack(moved + rotation, axis=0) / norm_root[None]

def reference(field_init, load, modulus, seg_z, seg_y, seg_x):
    table = jnp.asarray(hex_stiffness(), jnp.float32)
    total_z, total_y, width_x = modulus.shape
    keep = (jnp.arange(total_z) < total_z - 1)[:, None, None] & (jnp.arange(total_y) < total_y - 1)[None, :, None] & (jnp.arange(width_x) < width_x - 1)[None, None, :]
    masked = jnp.where(keep, modulus, jnp.float32(0.0))
    mod_pad = jnp.pad(masked, ((1, 1), (1, 1), (0, 0)))
    no_outside = jnp.zeros((CZ, total_y, width_x), jnp.float32)
    zero_index = jnp.int32(0)

    def pass_blocks(field, update):
        field_pad = jnp.pad(field, ((0, 0), (1, 1), (1, 1), (0, 0)))

        def one_block(index):
            anchor = (index * CZ).astype(jnp.int32)
            field_blk = lax.dynamic_slice(field_pad, (zero_index, anchor, zero_index, zero_index), (3, CZ + 2, total_y + 2, width_x))
            mod_blk = lax.dynamic_slice(mod_pad, (anchor, zero_index, zero_index), (CZ + 2, total_y + 2, width_x))
            load_blk = lax.dynamic_slice(load, (zero_index, anchor, zero_index, zero_index), (3, CZ, total_y, width_x))
            misfit = load_blk - apply_op(field_blk, mod_blk, table)
            if update:
                inverse = inverse_blocks(mod_blk, no_outside, table)
                return field_blk[:, 1:-1, 1:-1, :] + damping * block_mult(inverse, misfit)
            return misfit
        blocks = lax.map(one_block, jnp.arange(N_SLAB, dtype=jnp.int32))
        return jnp.moveaxis(blocks, 0, 1).reshape(3, total_z, total_y, width_x)
    field = field_init
    for sweep in range(SWEEPS):
        field = pass_blocks(field, True)
    residual = pass_blocks(field, False)
    seg_xx = seg_x.astype(jnp.int32)[None, None, :]
    seg_yy = seg_y.astype(jnp.int32)[None, :, None]
    seg_zz = seg_z.astype(jnp.int32)[:, None, None]
    place_x = jnp.arange(width_x, dtype=jnp.int32)[None, None, :]
    place_y = jnp.arange(total_y, dtype=jnp.int32)[None, :, None]
    place_z = jnp.arange(total_z, dtype=jnp.int32)[:, None, None]
    offset_x = 0.5 * (place_x - 4 * seg_xx - 2).astype(jnp.float32)
    offset_y = 0.5 * (place_y - 4 * seg_yy - 2).astype(jnp.float32)
    offset_z = 0.5 * (place_z - 4 * seg_zz - 2).astype(jnp.float32)
    terms = node_terms(residual, offset_x, offset_y, offset_z)
    ids = ((seg_zz * NSY + seg_yy) * SX + seg_xx).astype(jnp.int32)
    flat_ids = jnp.broadcast_to(ids, (total_z, total_y, width_x)).reshape(-1)
    sums = jnp.stack([jax.ops.segment_sum(term.reshape(-1), flat_ids, num_segments=NSZ * NSY * SX) for term in terms], axis=0)
    coarse = finalize(sums.reshape(10, NSZ, NSY, SX)).reshape(6, NSZ, NSY * SX)
    return (field, coarse)
```

```python
import functools

import jax
import jax.numpy as jnp
from jax import lax
from jax.experimental import pallas as pl
from jax.experimental.pallas import tpu as pltpu
from jax.sharding import PartitionSpec as P

SX = 32
SY = 4
SZ = 2
DEPTH = 8
ROWS = 16
WIDTH = 128
TALL = 24
DAMPING = 0.6

POISSON = 0.3
LAME = POISSON / ((1.0 + POISSON) * (1.0 - 2.0 * POISSON))
SHEAR = 0.5 / (1.0 + POISSON)

FIELD, LOAD, MODULUS = 0, 24, 48
PAIRS = 28
UP_PLANES = (
    [(FIELD, c, z) for c in range(3) for z in (5, 6, 7)]
    + [(LOAD, c, z) for c in range(3) for z in (6, 7)]
    + [(MODULUS, 0, z) for z in (5, 6, 7)]
)
DOWN_PLANES = (
    [(FIELD, c, z) for c in range(3) for z in (0, 1, 2, 3)]
    + [(LOAD, c, z) for c in range(3) for z in (0, 1, 2)]
    + [(MODULUS, 0, z) for z in (0, 1, 2)]
)


def y_slot(kind, c, z):
    index = kind + DEPTH * c + z
    return index // 2, 4 * (index % 2)


def is_even(axis):
    return lax.axis_index(axis) % 2 == 0


def pack_y(
    seg_y_hbm, seg_z_hbm, seg_x_hbm, field_hbm, load_hbm, modulus_hbm,
    first, second, field, load, modulus, labels, seg_y, seg_z, seg_x, sems,
):
    pairs = (
        (field_hbm, field), (load_hbm, load), (modulus_hbm, modulus),
        (seg_y_hbm, seg_y), (seg_z_hbm, seg_z), (seg_x_hbm, seg_x),
    )
    copies = [pltpu.make_async_copy(src, dst, sems.at[k]) for k, (src, dst) in enumerate(pairs)]
    for copy in copies:
        copy.start()
    even = is_even("sub")
    parts = ((field, FIELD, 3), (load, LOAD, 3), (modulus, MODULUS, 1))
    for copy, (ref, kind, comps) in zip(copies, parts):
        copy.wait()
        for c in range(comps):
            for z in range(DEPTH):
                tile, row = y_slot(kind, c, z)
                plane = ref[c, z] if comps == 3 else ref[z]
                up, down = plane[12:16], plane[0:4]
                first[tile, row : row + 4, :] = jnp.where(even, up, down)
                second[tile, row : row + 4, :] = jnp.where(even, down, up)
    for copy in copies[3:]:
        copy.wait()
    label = jnp.full((8, WIDTH), seg_y[0].astype(jnp.float32))
    first[PAIRS] = label
    second[PAIRS] = label
    for k in range(SY):
        labels[k : k + 1, :] = jnp.full((1, WIDTH), seg_y[4 * k].astype(jnp.float32))
    for k in range(SZ):
        labels[SY + k : SY + k + 1, :] = jnp.full((1, WIDTH), seg_z[4 * k].astype(jnp.float32))
    labels[7:8, :] = seg_x[...].reshape(1, WIDTH).astype(jnp.float32)


def edge_tile(even, first, second, kind, c, z):
    tile, row = y_slot(kind, c, z)
    one, two = first[tile, row : row + 4, :], second[tile, row : row + 4, :]
    above, below = jnp.where(even, one, two), jnp.where(even, two, one)
    return jnp.concatenate([above, below], axis=0)


def pack_z(labels, field, load, modulus, y_first, y_second, first, second):
    even_y, even_z = is_even("sub"), is_even("slab")
    tall = {}

    def whole(kind, c, z):
        if (kind, c, z) not in tall:
            own = (field if kind == FIELD else load)[c, z] if kind != MODULUS else modulus[z]
            tall[kind, c, z] = jnp.concatenate(
                [own, edge_tile(even_y, y_first, y_second, kind, c, z)], axis=0
            )
        return tall[kind, c, z]

    for index, plane in enumerate(DOWN_PLANES):
        down = whole(*plane)
        if index < len(UP_PLANES):
            up = whole(*UP_PLANES[index])
            first[index] = jnp.where(even_z, up, down)
            second[index] = jnp.where(even_z, down, up)
        else:
            first[index] = down
            second[index] = down
    label = jnp.broadcast_to(labels[SY : SY + 1, :], (TALL, WIDTH))
    first[len(DOWN_PLANES)] = label
    second[len(DOWN_PLANES)] = label


def roll_x(value, shift):
    return pltpu.roll(value, shift % WIDTH, 1)


def roll_y(value, shift):
    return pltpu.roll(value, shift % TALL, 0)


class Planes:
    def __init__(self, mine, offset, given=None):
        self.mine, self.offset, self.given = mine, offset, given
        self.written = set()

    def where(self, lead, z, tile, ref, offset):
        rows = slice(None) if tile is None else slice(8 * tile, 8 * tile + 8)
        return ref, (*lead, z + offset, rows, slice(None))

    def load(self, *lead, z, tile=None):
        own = {(*lead, z, t) in self.written for t in (range(3) if tile is None else (tile,))}
        assert len(own) == 1
        if own.pop():
            ref, at = self.where(lead, z, tile, self.mine, self.offset)
        else:
            ref, at = self.where(lead, z, tile, self.given, 0)
        return ref[at]

    def store(self, value, *lead, z, tile=None):
        self.written |= {(*lead, z, t) for t in (range(3) if tile is None else (tile,))}
        ref, at = self.where(lead, z, tile, self.mine, self.offset)
        ref[at] = value


def fill(state, even_y, blocks, y_first, y_second, z_first, z_second, planes):
    work, loads, elem = state[:3]
    field, load, modulus = blocks
    slab_pos, sub_pos = lax.axis_index("slab"), lax.axis_index("sub")
    last_slab, last_sub = lax.axis_size("slab") - 1, lax.axis_size("sub") - 1
    even_z = is_even("slab")

    def gather(kind, c, z, ref):
        if z < 0:
            index = UP_PLANES.index((kind, c, z + DEPTH))
            return jnp.where(even_z, z_second[index], z_first[index])
        if z >= DEPTH:
            index = DOWN_PLANES.index((kind, c, z - DEPTH))
            return jnp.where(even_z, z_first[index], z_second[index])
        own = ref[c, z] if kind != MODULUS else ref[z]
        return jnp.concatenate([own, edge_tile(even_y, y_first, y_second, kind, c, z)], axis=0)

    row = lax.broadcasted_iota(jnp.int32, (TALL, WIDTH), 0)
    lane = lax.broadcasted_iota(jnp.int32, (TALL, WIDTH), 1)
    inside = (lane < WIDTH - 1) & ((row != ROWS - 1) | (sub_pos != last_sub))
    inside_top = inside & (slab_pos != last_slab)
    for z in planes:
        if -3 <= z <= 10:
            value = gather(MODULUS, 0, z, modulus)
            elem.store(jnp.where(inside_top if z == DEPTH - 1 else inside, value, 0.0), z=z)
        for c in range(3):
            work.store(gather(FIELD, c, z, field), c, z=z)
            if -2 <= z <= 10:
                loads.store(gather(LOAD, c, z, load), c, z=z)


def invert(state, first, last):
    elem, inv = state[2], state[3]
    diag_scale = (LAME + 4.0 * SHEAR) / 9.0
    off_scale = (LAME + SHEAR) / 12.0
    before = None
    for z in range(first - 1, last + 1):
        e = elem.load(z=z)
        right = roll_x(e, 1)
        sum_x, dif_x = e + right, right - e
        sum_up, dif_up = roll_y(sum_x, 1), roll_y(dif_x, 1)
        now = (sum_up + sum_x, sum_up - sum_x, dif_up + dif_x, dif_up - dif_x)
        if before is not None:
            p = diag_scale * (before[0] + now[0])
            cc = off_scale * (before[1] - now[1])
            b = off_scale * (before[2] - now[2])
            a = off_scale * (before[3] + now[3])
            pp = p * p
            co00, co11, co22 = pp - cc * cc, pp - b * b, pp - a * a
            co01, co02, co12 = b * cc - a * p, a * cc - b * p, a * b - p * cc
            det = p * co00 + a * co01 + b * co02
            scale = jnp.where(det != 0.0, DAMPING / det, 0.0)
            for k, value in enumerate((co00, co01, co02, co11, co12, co22)):
                inv.store(value * scale, k, z=z)
        before = now


def spread(state, planes):
    work, modes = state[0], state[4]
    for c in range(3):
        for z in planes:
            v = work.load(c, z=z)
            left = roll_x(v, -1)
            sum_x, dif_x = v + left, left - v
            sum_up, dif_up = roll_y(sum_x, -1), roll_y(dif_x, -1)
            modes.store(sum_x + sum_up, 4 * c, z=z)
            modes.store(dif_x + dif_up, 4 * c + 1, z=z)
            modes.store(sum_up - sum_x, 4 * c + 2, z=z)
            modes.store(dif_up - dif_x, 4 * c + 3, z=z)


def stress(state, lo, hi, resume=False, join=False):
    elem, modes, forces = state[2], state[4], state[5]
    for tile in range(3):
        old = [modes.load(k, z=lo, tile=tile) for k in range(12)]
        held = [forces.load(k, z=lo, tile=tile) for k in range(12)] if resume else None
        for z in range(lo, hi):
            e = elem.load(z=z, tile=tile)
            new = [modes.load(k, z=z + 1, tile=tile) for k in range(12)]
            total = [None if k % 4 == 0 else new[k] + old[k] for k in range(12)]
            delta = [new[k] - old[k] for k in range(12)]
            xa, xb, xc = total[1], total[2], total[3]
            xd, xe, xf, xg = delta[0], delta[1], delta[2], delta[3]
            ya, yb, yc = total[5], total[6], total[7]
            yd, ye, yf, yg = delta[4], delta[5], delta[6], delta[7]
            za, zb, zc = total[9], total[10], total[11]
            zd, ze, zf, zg = delta[8], delta[9], delta[10], delta[11]
            lam0, mu0 = e * (LAME / 16.0), e * (SHEAR / 16.0)
            lam1, mu1 = e * (LAME / 48.0), e * (SHEAR / 48.0)
            twice = e * (SHEAR / 8.0)
            last_scale = e * ((LAME + 4.0 * SHEAR) / 144.0)
            t = lam0 * (xa + yb + zd)
            xy, xz, yz = mu0 * (xb + ya), mu0 * (xd + za), mu0 * (yd + zb)
            s_x, s_y, s_z = lam1 * (yc + ze), lam1 * (xc + zf), lam1 * (xe + yf)
            q = xf + ye + zc
            even = (
                None, t + twice * xa, xy, s_y + mu0 * xc,
                None, xy, t + twice * yb, s_x + mu0 * yc,
                None, xz, yz, mu1 * (q + zc),
            )
            odd = (
                xz, s_z + mu0 * xe, mu1 * (q + xf), last_scale * xg,
                yz, mu1 * (q + ye), s_z + mu0 * yf, last_scale * yg,
                t + twice * zd, s_x + mu0 * ze, s_y + mu0 * zf, last_scale * zg,
            )
            for k in range(12):
                low = -odd[k] if even[k] is None else even[k] - odd[k]
                forces.store(low if held is None else held[k] + low, k, z=z, tile=tile)
            held = [odd[k] if even[k] is None else even[k] + odd[k] for k in range(12)]
            old = new
        for k in range(12):
            total = forces.load(k, z=hi, tile=tile) + held[k] if join else held[k]
            forces.store(total, k, z=hi, tile=tile)


def misfit(state, z):
    loads, forces = state[1], state[5]
    out = []
    for c in range(3):
        f = [forces.load(4 * c + k, z=z) for k in range(4)]
        sum_x = (f[0] - f[2]) + roll_y(f[0] + f[2], 1)
        dif_x = (f[1] - f[3]) + roll_y(f[1] + f[3], 1)
        out.append(loads.load(c, z=z) - ((sum_x - dif_x) + roll_x(sum_x + dif_x, 1)))
    return out


def relax(state, planes):
    work, inv = state[0], state[3]
    table = ((0, 1, 2), (1, 3, 4), (2, 4, 5))
    for z in planes:
        m = [inv.load(k, z=z) for k in range(6)]
        r = misfit(state, z)
        for c in range(3):
            i, j, k = table[c]
            step = m[i] * r[0] + m[j] * r[1] + m[k] * r[2]
            work.store(work.load(c, z=z) + step, c, z=z)


def solve_inner(field, load, modulus, y_first, y_second, *refs):
    blocks = (field, load, modulus)
    state = [Planes(ref, 0) for ref in refs]
    fill(state, is_even("sub"), blocks, y_first, y_second, None, None, range(0, 8))
    invert(state, 1, 7)
    spread(state, range(0, 8))
    stress(state, 0, 7)
    relax(state, range(1, 7))
    spread(state, range(1, 7))
    stress(state, 1, 6)
    relax(state, range(2, 6))
    spread(state, range(2, 6))
    stress(state, 2, 5)


def solve_outer(
    labels, y_first, y_second, z_first, z_second, *refs
):
    smooth, coarse, rows = refs[6:9]
    state = [Planes(mine, 3, given) for given, mine in zip(refs[:6], refs[9:])]
    slab_pos, sub_pos = lax.axis_index("slab"), lax.axis_index("sub")
    last_slab, last_sub = lax.axis_size("slab") - 1, lax.axis_size("sub") - 1
    even_y, even_z = is_even("sub"), is_even("slab")
    row = lax.broadcasted_iota(jnp.int32, (TALL, WIDTH), 0)
    fill(state, even_y, (None,) * 3, y_first, y_second, z_first, z_second, [-3, -2, -1, 8, 9, 10, 11])
    invert(state, -2, 0)
    invert(state, 8, 10)
    for lo, hi, top in ((-3, 0, 11), (-2, 1, 10), (-1, 2, 9)):
        spread(state, list(range(lo, hi)) + list(range(8 - hi, top + 1)))
        stress(state, lo, hi, join=True)
        stress(state, 7 - hi, top, resume=True)
        if top > 9:
            relax(state, list(range(lo + 1, hi + 1)) + list(range(7 - hi, top)))
    work = state[0]
    for c in range(3):
        for z in range(DEPTH):
            smooth[c, z] = work.load(c, z=z)[:ROWS]

    def flag(value, segment):
        return jnp.where(value == segment.astype(jnp.float32), 1.0, 0.0)

    start_z = SZ * slab_pos
    owns_low = flag(labels[SY : SY + 1, :], start_z)
    mid_low = flag(labels[SY + 1 : SY + 2, :], start_z)
    mid_high = flag(labels[SY + 1 : SY + 2, :], start_z + 1)
    label = len(DOWN_PLANES)
    next_seg = jnp.where(even_z, z_first[label], z_second[label])[0:1]
    is_last_slab = slab_pos == last_slab
    owns_high = jnp.where(
        (next_seg == (start_z + 1).astype(jnp.float32)) & jnp.logical_not(is_last_slab), 1.0, 0.0
    )
    plane_weight = {
        (0, 0): owns_low, (0, 1): None, (0, 2): None, (0, 3): None, (0, 4): mid_low,
        (1, 4): mid_high, (1, 5): None, (1, 6): None, (1, 7): None, (1, 8): owns_high,
    }
    sums = [[None] * 5 for _ in range(SZ)]

    def restrict(z, r):
        for kz in range(SZ):
            if (kz, z) not in plane_weight:
                continue
            weight = plane_weight[kz, z]
            mine = r if weight is None else [weight * value for value in r]
            q = 0.5 * (z - 4 * kz - 2)
            terms = [mine[0], mine[1], mine[2], q * mine[1], q * mine[0]]
            for k in range(5):
                if k > 2 and q == 0.0:
                    continue
                sums[kz][k] = terms[k] if sums[kz][k] is None else sums[kz][k] + terms[k]

    for z in range(DEPTH + 1):
        restrict(z, misfit(state, z))
    count_z = [owns_low + 3.0 + mid_low, mid_high + 3.0 + owns_high]
    moment_z = [mid_low - owns_low, owns_high - mid_high]

    start_y = SY * sub_pos
    next_row = jnp.where(even_y, y_first[PAIRS], y_second[PAIRS])[0:1]
    owns_next = jnp.where(
        (next_row == (start_y + SY - 1).astype(jnp.float32)) & (sub_pos != last_sub), 1.0, 0.0
    )
    group = lax.broadcasted_iota(jnp.int32, (1, WIDTH), 1) // SX
    x = lax.broadcasted_iota(jnp.int32, (1, WIDTH), 1)
    seg_x = labels[7:8, :]
    q_x = 0.5 * (x.astype(jnp.float32) - 4.0 * seg_x - 2.0)
    count_y = jnp.zeros((1, WIDTH), jnp.float32)
    moment_y = jnp.zeros((1, WIDTH), jnp.float32)
    rows[...] = jnp.zeros((16 * SY, WIDTH), jnp.float32)
    for ky in range(SY):
        first = flag(labels[ky : ky + 1, :], start_y + ky)
        if ky < SY - 1:
            final = flag(labels[ky + 1 : ky + 2, :], start_y + ky)
        else:
            final = owns_next
        local = row - 4 * ky
        weight = jnp.where((local > 0) & (local < 4), 1.0, 0.0)
        weight = jnp.where(local == 0, first, jnp.where(local == 4, final, weight))
        moment = weight * (0.5 * (local - 2).astype(jnp.float32))
        count_y = jnp.where(group == ky, first + 3.0 + final, count_y)
        moment_y = jnp.where(group == ky, final - first, moment_y)
        total = lambda value: jnp.sum(value, axis=0, keepdims=True)
        for kz in range(SZ):
            r0, r1, r2, z1, z0 = sums[kz]
            plain = [total(weight * value) for value in (r0, r1, r2)]
            turned = [
                total(moment * r2 - weight * z1),
                total(weight * z0) - q_x * plain[2],
                q_x * plain[1] - total(moment * r0),
            ]
            for k, value in enumerate(plain + turned):
                rows[16 * ky + 6 * kz + k : 16 * ky + 6 * kz + k + 1, :] = value
        rows[16 * ky + 12 : 16 * ky + 13, :] = jnp.ones((1, WIDTH), jnp.float32)
        rows[16 * ky + 13 : 16 * ky + 14, :] = q_x

    target = lax.broadcasted_iota(jnp.int32, (WIDTH, WIDTH), 0) % SX
    chosen = jnp.where(target.astype(jnp.float32) == seg_x, 1.0, 0.0)
    totals = lax.dot_general(
        rows[...], chosen, (((1,), (1,)), ((), ())),
        precision=lax.Precision.HIGHEST, preferred_element_type=jnp.float32,
    )
    final_sums = totals[0:16]
    for ky in range(1, SY):
        final_sums = jnp.where(group == ky, totals[16 * ky : 16 * ky + 16], final_sums)
    count_x, moment_x = final_sums[12:13], final_sums[13:14]
    for kz in range(SZ):
        count = count_x * count_y * count_z[kz]
        centre = [
            moment_x * count_y * count_z[kz] / count,
            count_x * moment_y * count_z[kz] / count,
            count_x * count_y * moment_z[kz] / count,
        ]
        scale = 1.0 / jnp.sqrt(count)
        s = [final_sums[6 * kz + k : 6 * kz + k + 1] for k in range(6)]
        turned = [
            s[3] - (centre[1] * s[2] - centre[2] * s[1]),
            s[4] - (centre[2] * s[0] - centre[0] * s[2]),
            s[5] - (centre[0] * s[1] - centre[1] * s[0]),
        ]
        for k, value in enumerate(s[:3] + turned):
            coarse[k, kz : kz + 1, :] = value * scale


VMEM = pl.BlockSpec(memory_space=pltpu.VMEM)


def f32(*shape):
    return jax.ShapeDtypeStruct(shape, jnp.float32)


def scratch(*shape):
    return pltpu.VMEM(shape, jnp.float32)


def on_device(field_init, load, modulus, seg_z, seg_y, seg_x):
    def exchange(first, second, axis):
        count = lax.axis_size(axis)
        outcome = []
        for block, start in ((second, 1), (first, 0)):
            pairs = [(i, i + 1) for i in range(start, count - 1, 2)]
            outcome.append(lax.ppermute(block, axis, pairs + [(j, i) for i, j in pairs]))
        return outcome[1], outcome[0]

    def limit(mib):
        return pltpu.CompilerParams(vmem_limit_bytes=mib << 20)

    hbm = pl.BlockSpec(memory_space=pltpu.MemorySpace.HBM)
    blocks = [f32(3, DEPTH, ROWS, WIDTH), f32(3, DEPTH, ROWS, WIDTH), f32(DEPTH, ROWS, WIDTH)]
    arguments = (seg_y, seg_z, seg_x, field_init, load, modulus)
    *packed, field_init, load, modulus, labels = pl.pallas_call(
        pack_y,
        out_shape=[f32(PAIRS + 1, 8, WIDTH)] * 2 + blocks + [f32(8, WIDTH)],
        in_specs=[hbm] * 6,
        out_specs=[VMEM] * 6,
        scratch_shapes=[
            pltpu.SMEM((ROWS,), jnp.int32),
            pltpu.SMEM((DEPTH,), jnp.int32),
            pltpu.VMEM((WIDTH,), jnp.int32),
            pltpu.SemaphoreType.DMA((6,)),
        ],
        compiler_params=limit(4),
        name="pack_y",
    )(*[pltpu.with_memory_space_constraint(value, pltpu.MemorySpace.HBM) for value in arguments])
    y_parts = exchange(*packed, "sub")
    packed = pl.pallas_call(
        pack_z,
        out_shape=(f32(len(DOWN_PLANES) + 1, TALL, WIDTH),) * 2,
        in_specs=[VMEM] * 6,
        out_specs=(VMEM, VMEM),
        compiler_params=limit(4),
        name="pack_z",
    )(labels, field_init, load, modulus, *y_parts)
    z_parts = exchange(*packed, "slab")
    def sizes(planes):
        return [(3, planes, TALL, WIDTH)] * 2 + [(planes, TALL, WIDTH)] + [
            (n, planes, TALL, WIDTH) for n in (6, 12, 12)
        ]

    state = pl.pallas_call(
        solve_inner,
        out_shape=[f32(*size) for size in sizes(DEPTH)],
        in_specs=[VMEM] * 5,
        out_specs=[VMEM] * 6,
        compiler_params=limit(6),
        name="solve_inner",
    )(field_init, load, modulus, *y_parts)
    return pl.pallas_call(
        solve_outer,
        out_shape=(f32(3, DEPTH, ROWS, WIDTH), f32(6, SZ, SY * SX)),
        in_specs=[VMEM] * 11,
        out_specs=(VMEM, VMEM),
        scratch_shapes=[scratch(16 * SY, WIDTH)] + [scratch(*size) for size in sizes(15)],
        compiler_params=limit(12),
        name="solve_outer",
    )(labels, *y_parts, *z_parts, *state)


def solution(mesh):
    in_specs = (
        P(None, "slab", "sub", None),
        P(None, "slab", "sub", None),
        P("slab", "sub", None),
        P("slab"),
        P("sub"),
        P(),
    )
    out_specs = (P(None, "slab", "sub", None), P(None, "slab", "sub"))
    return jax.shard_map(
        on_device, mesh=mesh, in_specs=in_specs, out_specs=out_specs, check_vma=False
    )
```

```python
import jax
import jax.numpy as jnp
from jax import lax
from jax.experimental import pallas as pl
from jax.experimental.pallas import tpu as pltpu
from jax.sharding import PartitionSpec as P


SX = 32
SY = 4
SZ = 2
DEPTH = 8
ROWS = 16
WIDTH = 128
TALL = 24
DAMPING = 0.6

POISSON = 0.3
LAME = POISSON / ((1.0 + POISSON) * (1.0 - 2.0 * POISSON))
SHEAR = 0.5 / (1.0 + POISSON)

FIELD, LOAD, MODULUS = 0, 24, 48
PAIRS = 28
UP_PLANES = (
    [(FIELD, c, z) for c in range(3) for z in (5, 6, 7)]
    + [(LOAD, c, z) for c in range(3) for z in (6, 7)]
    + [(MODULUS, 0, z) for z in (5, 6, 7)]
)
DOWN_PLANES = (
    [(FIELD, c, z) for c in range(3) for z in (0, 1, 2, 3)]
    + [(LOAD, c, z) for c in range(3) for z in (0, 1, 2)]
    + [(MODULUS, 0, z) for z in (0, 1, 2)]
)


def y_slot(kind, c, z):
    index = kind + DEPTH * c + z
    return index // 2, 4 * (index % 2)


def is_even(axis):
    return lax.axis_index(axis) % 2 == 0


def pack_y(
    seg_y_hbm, seg_z_hbm, seg_x_hbm, field_hbm, load_hbm, modulus_hbm,
    first, second, field, load, modulus, labels, seg_y, seg_z, seg_x, sems,
):
    pairs = (
        (field_hbm, field), (load_hbm, load), (modulus_hbm, modulus),
        (seg_y_hbm, seg_y), (seg_z_hbm, seg_z), (seg_x_hbm, seg_x),
    )
    copies = [pltpu.make_async_copy(src, dst, sems.at[k]) for k, (src, dst) in enumerate(pairs)]
    for copy in copies:
        copy.start()
    even = is_even("sub")
    parts = ((field, FIELD, 3), (load, LOAD, 3), (modulus, MODULUS, 1))
    for copy, (ref, kind, comps) in zip(copies, parts):
        copy.wait()
        for c in range(comps):
            for z in range(DEPTH):
                tile, row = y_slot(kind, c, z)
                plane = ref[c, z] if comps == 3 else ref[z]
                up, down = plane[12:16], plane[0:4]
                first[tile, row : row + 4, :] = jnp.where(even, up, down)
                second[tile, row : row + 4, :] = jnp.where(even, down, up)
    for copy in copies[3:]:
        copy.wait()
    label = jnp.full((8, WIDTH), seg_y[0].astype(jnp.float32))
    first[PAIRS] = label
    second[PAIRS] = label
    for k in range(SY):
        labels[k : k + 1, :] = jnp.full((1, WIDTH), seg_y[4 * k].astype(jnp.float32))
    for k in range(SZ):
        labels[SY + k : SY + k + 1, :] = jnp.full((1, WIDTH), seg_z[4 * k].astype(jnp.float32))
    labels[7:8, :] = seg_x[...].reshape(1, WIDTH).astype(jnp.float32)


def edge_tile(even, first, second, kind, c, z):
    tile, row = y_slot(kind, c, z)
    one, two = first[tile, row : row + 4, :], second[tile, row : row + 4, :]
    above, below = jnp.where(even, one, two), jnp.where(even, two, one)
    return jnp.concatenate([above, below], axis=0)


def pack_z(labels, field, load, modulus, y_first, y_second, first, second):
    even_y, even_z = is_even("sub"), is_even("slab")
    tall = {}

    def whole(kind, c, z):
        if (kind, c, z) not in tall:
            own = (field if kind == FIELD else load)[c, z] if kind != MODULUS else modulus[z]
            tall[kind, c, z] = jnp.concatenate(
                [own, edge_tile(even_y, y_first, y_second, kind, c, z)], axis=0
            )
        return tall[kind, c, z]

    for index, plane in enumerate(DOWN_PLANES):
        down = whole(*plane)
        if index < len(UP_PLANES):
            up = whole(*UP_PLANES[index])
            first[index] = jnp.where(even_z, up, down)
            second[index] = jnp.where(even_z, down, up)
        else:
            first[index] = down
            second[index] = down
    label = jnp.broadcast_to(labels[SY : SY + 1, :], (TALL, WIDTH))
    first[len(DOWN_PLANES)] = label
    second[len(DOWN_PLANES)] = label


def roll_x(value, shift):
    return pltpu.roll(value, shift % WIDTH, 1)


def roll_y(value, shift):
    return pltpu.roll(value, shift % TALL, 0)


class Planes:
    def __init__(self, mine, offset, given=None):
        self.mine, self.offset, self.given = mine, offset, given
        self.written = set()

    def where(self, lead, z, tile, ref, offset):
        rows = slice(None) if tile is None else slice(8 * tile, 8 * tile + 8)
        return ref, (*lead, z + offset, rows, slice(None))

    def load(self, *lead, z, tile=None):
        own = {(*lead, z, t) in self.written for t in (range(3) if tile is None else (tile,))}
        assert len(own) == 1
        if own.pop():
            ref, at = self.where(lead, z, tile, self.mine, self.offset)
        else:
            ref, at = self.where(lead, z, tile, self.given, 0)
        return ref[at]

    def store(self, value, *lead, z, tile=None):
        self.written |= {(*lead, z, t) for t in (range(3) if tile is None else (tile,))}
        ref, at = self.where(lead, z, tile, self.mine, self.offset)
        ref[at] = value


def fill(state, planes, own_block=None, z_part=None):
    work, loads, elem = state[:3]
    slab_pos, sub_pos = lax.axis_index("slab"), lax.axis_index("sub")
    last_slab, last_sub = lax.axis_size("slab") - 1, lax.axis_size("sub") - 1

    def gather(kind, c, z):
        if z < 0:
            return z_part[UP_PLANES.index((kind, c, z + DEPTH))]
        if z >= DEPTH:
            return z_part[DOWN_PLANES.index((kind, c, z - DEPTH))]
        field, load, modulus, y_first, y_second = own_block
        own = (field if kind == FIELD else load)[c, z] if kind != MODULUS else modulus[z]
        return jnp.concatenate([own, edge_tile(is_even("sub"), y_first, y_second, kind, c, z)], axis=0)

    row = lax.broadcasted_iota(jnp.int32, (TALL, WIDTH), 0)
    lane = lax.broadcasted_iota(jnp.int32, (TALL, WIDTH), 1)
    inside = (lane < WIDTH - 1) & ((row != ROWS - 1) | (sub_pos != last_sub))
    inside_top = inside & (slab_pos != last_slab)
    for z in planes:
        if -3 <= z <= 10:
            value = gather(MODULUS, 0, z)
            elem.store(jnp.where(inside_top if z == DEPTH - 1 else inside, value, 0.0), z=z)
        for c in range(3):
            work.store(gather(FIELD, c, z), c, z=z)
            if -2 <= z <= 10:
                loads.store(gather(LOAD, c, z), c, z=z)


def invert(state, first, last):
    elem, inv = state[2], state[3]
    diag_scale = (LAME + 4.0 * SHEAR) / 9.0
    off_scale = (LAME + SHEAR) / 12.0
    before = None
    for z in range(first - 1, last + 1):
        e = elem.load(z=z)
        right = roll_x(e, 1)
        sum_x, dif_x = e + right, right - e
        sum_up, dif_up = roll_y(sum_x, 1), roll_y(dif_x, 1)
        now = (sum_up + sum_x, sum_up - sum_x, dif_up + dif_x, dif_up - dif_x)
        if before is not None:
            p = diag_scale * (before[0] + now[0])
            cc = off_scale * (before[1] - now[1])
            b = off_scale * (before[2] - now[2])
            a = off_scale * (before[3] + now[3])
            pp = p * p
            co00, co11, co22 = pp - cc * cc, pp - b * b, pp - a * a
            co01, co02, co12 = b * cc - a * p, a * cc - b * p, a * b - p * cc
            det = p * co00 + a * co01 + b * co02
            scale = jnp.where(det != 0.0, DAMPING / det, 0.0)
            for k, value in enumerate((co00, co01, co02, co11, co12, co22)):
                inv.store(value * scale, k, z=z)
        before = now


def spread(state, planes):
    work, modes = state[0], state[4]
    for c in range(3):
        for z in planes:
            v = work.load(c, z=z)
            left = roll_x(v, -1)
            sum_x, dif_x = v + left, left - v
            sum_up, dif_up = roll_y(sum_x, -1), roll_y(dif_x, -1)
            modes.store(sum_x + sum_up, 4 * c, z=z)
            modes.store(dif_x + dif_up, 4 * c + 1, z=z)
            modes.store(sum_up - sum_x, 4 * c + 2, z=z)
            modes.store(dif_up - dif_x, 4 * c + 3, z=z)


def stress(state, lo, hi, resume=False, join=False):
    elem, modes, forces = state[2], state[4], state[5]
    for tile in range(3):
        old = [modes.load(k, z=lo, tile=tile) for k in range(12)]
        held = [forces.load(k, z=lo, tile=tile) for k in range(12)] if resume else None
        for z in range(lo, hi):
            e = elem.load(z=z, tile=tile)
            new = [modes.load(k, z=z + 1, tile=tile) for k in range(12)]
            total = [None if k % 4 == 0 else new[k] + old[k] for k in range(12)]
            delta = [new[k] - old[k] for k in range(12)]
            xa, xb, xc = total[1], total[2], total[3]
            xd, xe, xf, xg = delta[0], delta[1], delta[2], delta[3]
            ya, yb, yc = total[5], total[6], total[7]
            yd, ye, yf, yg = delta[4], delta[5], delta[6], delta[7]
            za, zb, zc = total[9], total[10], total[11]
            zd, ze, zf, zg = delta[8], delta[9], delta[10], delta[11]
            lam0, mu0 = e * (LAME / 16.0), e * (SHEAR / 16.0)
            lam1, mu1 = e * (LAME / 48.0), e * (SHEAR / 48.0)
            twice = e * (SHEAR / 8.0)
            last_scale = e * ((LAME + 4.0 * SHEAR) / 144.0)
            t = lam0 * (xa + yb + zd)
            xy, xz, yz = mu0 * (xb + ya), mu0 * (xd + za), mu0 * (yd + zb)
            s_x, s_y, s_z = lam1 * (yc + ze), lam1 * (xc + zf), lam1 * (xe + yf)
            q = xf + ye + zc
            even = (
                None, t + twice * xa, xy, s_y + mu0 * xc,
                None, xy, t + twice * yb, s_x + mu0 * yc,
                None, xz, yz, mu1 * (q + zc),
            )
            odd = (
                xz, s_z + mu0 * xe, mu1 * (q + xf), last_scale * xg,
                yz, mu1 * (q + ye), s_z + mu0 * yf, last_scale * yg,
                t + twice * zd, s_x + mu0 * ze, s_y + mu0 * zf, last_scale * zg,
            )
            for k in range(12):
                low = -odd[k] if even[k] is None else even[k] - odd[k]
                forces.store(low if held is None else held[k] + low, k, z=z, tile=tile)
            held = [odd[k] if even[k] is None else even[k] + odd[k] for k in range(12)]
            old = new
        for k in range(12):
            total = forces.load(k, z=hi, tile=tile) + held[k] if join else held[k]
            forces.store(total, k, z=hi, tile=tile)


def misfit(state, z):
    loads, forces = state[1], state[5]
    out = []
    for c in range(3):
        f = [forces.load(4 * c + k, z=z) for k in range(4)]
        sum_x = (f[0] - f[2]) + roll_y(f[0] + f[2], 1)
        dif_x = (f[1] - f[3]) + roll_y(f[1] + f[3], 1)
        out.append(loads.load(c, z=z) - ((sum_x - dif_x) + roll_x(sum_x + dif_x, 1)))
    return out


def relax(state, planes):
    work, inv = state[0], state[3]
    table = ((0, 1, 2), (1, 3, 4), (2, 4, 5))
    for z in planes:
        m = [inv.load(k, z=z) for k in range(6)]
        r = misfit(state, z)
        for c in range(3):
            i, j, k = table[c]
            step = m[i] * r[0] + m[j] * r[1] + m[k] * r[2]
            work.store(work.load(c, z=z) + step, c, z=z)


def solve_inner(field, load, modulus, y_first, y_second, *refs):
    state = [Planes(ref, 0) for ref in refs[:6]]
    residual = refs[6]
    fill(state, range(0, 8), own_block=(field, load, modulus, y_first, y_second))
    invert(state, 1, 7)
    spread(state, range(0, 8))
    stress(state, 0, 7)
    relax(state, range(1, 7))
    spread(state, range(1, 7))
    stress(state, 1, 6)
    relax(state, range(2, 6))
    spread(state, range(2, 6))
    stress(state, 2, 5)
    for z in (3, 4):
        for c, value in enumerate(misfit(state, z)):
            residual[c, z - 3] = value


LOWER, UPPER = (0, 1), (6, 7)
LOWER_REST, UPPER_REST = (0, 1, 2), (5, 6, 7, 8)


def solve_side(lower, z_part, given, mine, smooth, residual, smooth_from, residual_from):
    state = [Planes(ref, 3, old) for ref, old in zip(mine, given)]
    if lower:
        fill(state, range(-3, 0), z_part=z_part)
        invert(state, -2, 0)
        for first, last in ((-3, 0), (-2, 1), (-1, 2)):
            spread(state, range(first, last))
            stress(state, first, last, join=True)
            if last < 2:
                relax(state, range(first + 1, last + 1))
    else:
        fill(state, range(8, 12), z_part=z_part)
        invert(state, 8, 10)
        for first, last in ((7, 11), (6, 10), (5, 9)):
            spread(state, range(first + 1, last + 1))
            stress(state, first, last, resume=True)
            if last > 9:
                relax(state, range(first, last))
    for k, z in enumerate(LOWER if lower else UPPER):
        for c in range(3):
            smooth[c, smooth_from + k] = state[0].load(c, z=z)[:ROWS]
    for k, z in enumerate(LOWER_REST if lower else UPPER_REST):
        for c, value in enumerate(misfit(state, z)):
            residual[c, residual_from + k] = value


def solve_near(z_first, *refs):
    given, (smooth, residual), mine = refs[:6], refs[6:8], refs[8:14]
    for lower in (False, True):

        @pl.when(is_even("slab") != lower)
        def side():
            solve_side(lower, z_first, given, mine, smooth, residual, 0, 0)


def solve_far(labels, y_first, y_second, z_first, z_second, *refs):
    given, (middle, near_smooth, near_residual) = refs[:6], refs[6:9]
    (smooth, coarse), rows, residual, mine = refs[9:11], refs[11], refs[12], refs[13:19]
    slab_pos, sub_pos = lax.axis_index("slab"), lax.axis_index("sub")
    last_slab, last_sub = lax.axis_size("slab") - 1, lax.axis_size("sub") - 1
    even_y, even_z = is_even("sub"), is_even("slab")
    row = lax.broadcasted_iota(jnp.int32, (TALL, WIDTH), 0)
    for lower in (True, False):

        @pl.when(even_z == lower)
        def side():
            far, far_rest = (LOWER, LOWER_REST) if lower else (UPPER, UPPER_REST)
            near, near_rest = (UPPER, UPPER_REST) if lower else (LOWER, LOWER_REST)
            solve_side(lower, z_second, given, mine, smooth, residual, far[0], far_rest[0])
            for c in range(3):
                for k, z in enumerate(near):
                    smooth[c, z] = near_smooth[c, k]
                for k, z in enumerate(near_rest):
                    residual[c, z] = near_residual[c, k]

    for c in range(3):
        for z in range(2, 6):
            smooth[c, z] = given[0][c, z, :ROWS, :]
        for k in range(2):
            residual[c, 3 + k] = middle[c, k]

    def flag(value, segment):
        return jnp.where(value == segment.astype(jnp.float32), 1.0, 0.0)

    start_z = SZ * slab_pos
    owns_low = flag(labels[SY : SY + 1, :], start_z)
    mid_low = flag(labels[SY + 1 : SY + 2, :], start_z)
    mid_high = flag(labels[SY + 1 : SY + 2, :], start_z + 1)
    label = len(DOWN_PLANES)
    next_seg = jnp.where(even_z, z_first[label], z_second[label])[0:1]
    is_last_slab = slab_pos == last_slab
    owns_high = jnp.where(
        (next_seg == (start_z + 1).astype(jnp.float32)) & jnp.logical_not(is_last_slab), 1.0, 0.0
    )
    plane_weight = {
        (0, 0): owns_low, (0, 1): None, (0, 2): None, (0, 3): None, (0, 4): mid_low,
        (1, 4): mid_high, (1, 5): None, (1, 6): None, (1, 7): None, (1, 8): owns_high,
    }
    sums = [[None] * 5 for _ in range(SZ)]

    def restrict(z, r):
        for kz in range(SZ):
            if (kz, z) not in plane_weight:
                continue
            weight = plane_weight[kz, z]
            mine = r if weight is None else [weight * value for value in r]
            q = 0.5 * (z - 4 * kz - 2)
            terms = [mine[0], mine[1], mine[2], q * mine[1], q * mine[0]]
            for k in range(5):
                if k > 2 and q == 0.0:
                    continue
                sums[kz][k] = terms[k] if sums[kz][k] is None else sums[kz][k] + terms[k]

    for z in range(DEPTH + 1):
        restrict(z, [residual[c, z] for c in range(3)])
    count_z = [owns_low + 3.0 + mid_low, mid_high + 3.0 + owns_high]
    moment_z = [mid_low - owns_low, owns_high - mid_high]

    start_y = SY * sub_pos
    next_row = jnp.where(even_y, y_first[PAIRS], y_second[PAIRS])[0:1]
    owns_next = jnp.where(
        (next_row == (start_y + SY - 1).astype(jnp.float32)) & (sub_pos != last_sub), 1.0, 0.0
    )
    group = lax.broadcasted_iota(jnp.int32, (1, WIDTH), 1) // SX
    x = lax.broadcasted_iota(jnp.int32, (1, WIDTH), 1)
    seg_x = labels[7:8, :]
    q_x = 0.5 * (x.astype(jnp.float32) - 4.0 * seg_x - 2.0)
    count_y = jnp.zeros((1, WIDTH), jnp.float32)
    moment_y = jnp.zeros((1, WIDTH), jnp.float32)
    rows[...] = jnp.zeros((16 * SY, WIDTH), jnp.float32)
    for ky in range(SY):
        first = flag(labels[ky : ky + 1, :], start_y + ky)
        if ky < SY - 1:
            final = flag(labels[ky + 1 : ky + 2, :], start_y + ky)
        else:
            final = owns_next
        local = row - 4 * ky
        weight = jnp.where((local > 0) & (local < 4), 1.0, 0.0)
        weight = jnp.where(local == 0, first, jnp.where(local == 4, final, weight))
        moment = weight * (0.5 * (local - 2).astype(jnp.float32))
        count_y = jnp.where(group == ky, first + 3.0 + final, count_y)
        moment_y = jnp.where(group == ky, final - first, moment_y)
        total = lambda value: jnp.sum(value, axis=0, keepdims=True)
        for kz in range(SZ):
            r0, r1, r2, z1, z0 = sums[kz]
            plain = [total(weight * value) for value in (r0, r1, r2)]
            turned = [
                total(moment * r2 - weight * z1),
                total(weight * z0) - q_x * plain[2],
                q_x * plain[1] - total(moment * r0),
            ]
            for k, value in enumerate(plain + turned):
                rows[16 * ky + 6 * kz + k : 16 * ky + 6 * kz + k + 1, :] = value
        rows[16 * ky + 12 : 16 * ky + 13, :] = jnp.ones((1, WIDTH), jnp.float32)
        rows[16 * ky + 13 : 16 * ky + 14, :] = q_x

    target = lax.broadcasted_iota(jnp.int32, (WIDTH, WIDTH), 0) % SX
    chosen = jnp.where(target.astype(jnp.float32) == seg_x, 1.0, 0.0)
    totals = lax.dot_general(
        rows[...], chosen, (((1,), (1,)), ((), ())),
        precision=lax.Precision.HIGHEST, preferred_element_type=jnp.float32,
    )
    final_sums = totals[0:16]
    for ky in range(1, SY):
        final_sums = jnp.where(group == ky, totals[16 * ky : 16 * ky + 16], final_sums)
    count_x, moment_x = final_sums[12:13], final_sums[13:14]
    for kz in range(SZ):
        count = count_x * count_y * count_z[kz]
        centre = [
            moment_x * count_y * count_z[kz] / count,
            count_x * moment_y * count_z[kz] / count,
            count_x * count_y * moment_z[kz] / count,
        ]
        scale = 1.0 / jnp.sqrt(count)
        s = [final_sums[6 * kz + k : 6 * kz + k + 1] for k in range(6)]
        turned = [
            s[3] - (centre[1] * s[2] - centre[2] * s[1]),
            s[4] - (centre[2] * s[0] - centre[0] * s[2]),
            s[5] - (centre[0] * s[1] - centre[1] * s[0]),
        ]
        for k, value in enumerate(s[:3] + turned):
            coarse[k, kz : kz + 1, :] = value * scale


VMEM = pl.BlockSpec(memory_space=pltpu.VMEM)


def f32(*shape):
    return jax.ShapeDtypeStruct(shape, jnp.float32)


def scratch(*shape):
    return pltpu.VMEM(shape, jnp.float32)


def on_device(field_init, load, modulus, seg_z, seg_y, seg_x):
    def exchange(first, second, axis):
        count = lax.axis_size(axis)
        outcome = []
        for block, start in ((second, 1), (first, 0)):
            pairs = [(i, i + 1) for i in range(start, count - 1, 2)]
            outcome.append(lax.ppermute(block, axis, pairs + [(j, i) for i, j in pairs]))
        return outcome[1], outcome[0]

    def limit(mib):
        return pltpu.CompilerParams(vmem_limit_bytes=mib << 20)

    hbm = pl.BlockSpec(memory_space=pltpu.MemorySpace.HBM)
    blocks = [f32(3, DEPTH, ROWS, WIDTH), f32(3, DEPTH, ROWS, WIDTH), f32(DEPTH, ROWS, WIDTH)]
    arguments = (seg_y, seg_z, seg_x, field_init, load, modulus)
    *packed, field_init, load, modulus, labels = pl.pallas_call(
        pack_y,
        out_shape=[f32(PAIRS + 1, 8, WIDTH)] * 2 + blocks + [f32(8, WIDTH)],
        in_specs=[hbm] * 6,
        out_specs=[VMEM] * 6,
        scratch_shapes=[
            pltpu.SMEM((ROWS,), jnp.int32),
            pltpu.SMEM((DEPTH,), jnp.int32),
            pltpu.VMEM((WIDTH,), jnp.int32),
            pltpu.SemaphoreType.DMA((6,)),
        ],
        compiler_params=limit(4),
        name="pack_y",
    )(*[pltpu.with_memory_space_constraint(value, pltpu.MemorySpace.HBM) for value in arguments])
    y_parts = exchange(*packed, "sub")
    packed = pl.pallas_call(
        pack_z,
        out_shape=(f32(len(DOWN_PLANES) + 1, TALL, WIDTH),) * 2,
        in_specs=[VMEM] * 6,
        out_specs=(VMEM, VMEM),
        compiler_params=limit(4),
        name="pack_z",
    )(labels, field_init, load, modulus, *y_parts)
    z_parts = exchange(*packed, "slab")

    def sizes(planes):
        return [(3, planes, TALL, WIDTH)] * 2 + [(planes, TALL, WIDTH)] + [
            (n, planes, TALL, WIDTH) for n in (6, 12, 12)
        ]

    *state, middle = pl.pallas_call(
        solve_inner,
        out_shape=[f32(*size) for size in sizes(DEPTH)] + [f32(3, 2, TALL, WIDTH)],
        in_specs=[VMEM] * 5,
        out_specs=[VMEM] * 7,
        compiler_params=limit(6),
        name="solve_inner",
    )(field_init, load, modulus, *y_parts)
    near = pl.pallas_call(
        solve_near,
        out_shape=(f32(3, 2, ROWS, WIDTH), f32(3, 4, TALL, WIDTH)),
        in_specs=[VMEM] * 7,
        out_specs=(VMEM, VMEM),
        scratch_shapes=[scratch(*size) for size in sizes(15)],
        compiler_params=limit(12),
        name="solve_near",
    )(z_parts[0], *state)
    return pl.pallas_call(
        solve_far,
        out_shape=(f32(3, DEPTH, ROWS, WIDTH), f32(6, SZ, SY * SX)),
        in_specs=[VMEM] * 14,
        out_specs=(VMEM, VMEM),
        scratch_shapes=[scratch(16 * SY, WIDTH), scratch(3, 9, TALL, WIDTH)]
        + [scratch(*size) for size in sizes(15)],
        compiler_params=limit(14),
        name="solve_far",
    )(labels, *y_parts, *z_parts, *state, middle, *near)


def solution(mesh):
    in_specs = (
        P(None, "slab", "sub", None),
        P(None, "slab", "sub", None),
        P("slab", "sub", None),
        P("slab"),
        P("sub"),
        P(),
    )
    out_specs = (P(None, "slab", "sub", None), P(None, "slab", "sub"))
    return jax.shard_map(
        on_device, mesh=mesh, in_specs=in_specs, out_specs=out_specs, check_vma=False
    )
```

```python
import functools

import jax
import jax.numpy as jnp
from jax import lax
from jax.experimental import pallas as pl
from jax.experimental.pallas import tpu as pltpu
from jax.sharding import PartitionSpec as P


SX = 32
SY = 4
SZ = 2
DEPTH = 8
ROWS = 16
WIDTH = 128
TALL = 24
DAMPING = 0.6

POISSON = 0.3
LAME = POISSON / ((1.0 + POISSON) * (1.0 - 2.0 * POISSON))
SHEAR = 0.5 / (1.0 + POISSON)

FIELD, LOAD, MODULUS = 0, 1, 2
UP_ROWS, DOWN_ROWS = (3, 2, 3), (4, 3, 3)
UP_AT, DOWN_AT = (0, 72, 120), (0, 96, 168)
UP_SIZE, DOWN_SIZE = 144, 192
UP_PLANES = (
    [(FIELD, c, z) for c in range(3) for z in (5, 6, 7)]
    + [(LOAD, c, z) for c in range(3) for z in (6, 7)]
    + [(MODULUS, 0, z) for z in (5, 6, 7)]
)
DOWN_PLANES = (
    [(FIELD, c, z) for c in range(3) for z in (0, 1, 2, 3)]
    + [(LOAD, c, z) for c in range(3) for z in (0, 1, 2)]
    + [(MODULUS, 0, z) for z in (0, 1, 2)]
)


LABEL_PLANE = (MODULUS, 0, 0)


def y_rows(kind, c, z, up):
    rows, start = (UP_ROWS[kind], UP_AT[kind]) if up else (DOWN_ROWS[kind], DOWN_AT[kind])
    start += rows * (DEPTH * c + z)
    return slice(start, start + rows)


def is_even(axis):
    return lax.axis_index(axis) % 2 == 0


def pack_y(
    seg_y_hbm, seg_z_hbm, seg_x_hbm, field_hbm, load_hbm, modulus_hbm,
    up, down, field, load, modulus, labels, seg_y, seg_z, seg_x, sems,
):
    pairs = (
        (field_hbm, field), (load_hbm, load), (modulus_hbm, modulus),
        (seg_y_hbm, seg_y), (seg_z_hbm, seg_z), (seg_x_hbm, seg_x),
    )
    copies = [pltpu.make_async_copy(src, dst, sems.at[k]) for k, (src, dst) in enumerate(pairs)]
    for copy in copies:
        copy.start()
    for copy, ref, kind in zip(copies, (field, load, modulus), (FIELD, LOAD, MODULUS)):
        copy.wait()
        for c in range(1 if kind == MODULUS else 3):
            for z in range(DEPTH):
                at = (z,) if kind == MODULUS else (c, z)
                up[y_rows(kind, c, z, True), :] = ref[(*at, slice(ROWS - UP_ROWS[kind], ROWS), slice(None))]
                down[y_rows(kind, c, z, False), :] = ref[(*at, slice(0, DOWN_ROWS[kind]), slice(None))]
    for copy in copies[3:]:
        copy.wait()
    down[DOWN_SIZE:, :] = jnp.full((8, WIDTH), seg_y[0].astype(jnp.float32))
    for k in range(SY):
        labels[k : k + 1, :] = jnp.full((1, WIDTH), seg_y[4 * k].astype(jnp.float32))
    for k in range(SZ):
        labels[SY + k : SY + k + 1, :] = jnp.full((1, WIDTH), seg_z[4 * k].astype(jnp.float32))
    labels[7:8, :] = seg_x[...].reshape(1, WIDTH).astype(jnp.float32)


def edge_tile(below, above, kind, c, z):
    parts = [above[y_rows(kind, c, z, False), :]]
    spare = 8 - UP_ROWS[kind] - DOWN_ROWS[kind]
    parts.append(jnp.zeros((spare, WIDTH), jnp.float32))
    parts.append(below[y_rows(kind, c, z, True), :])
    return jnp.concatenate(parts, axis=0)


def pack_z(labels, field, load, modulus, y_below, y_above, first, second):
    even = is_even("slab")
    lane = lax.broadcasted_iota(jnp.int32, (TALL, WIDTH), 1)
    tall = {}

    def whole(kind, c, z):
        if (kind, c, z) not in tall:
            own = (field if kind == FIELD else load)[c, z] if kind != MODULUS else modulus[z]
            tall[kind, c, z] = jnp.concatenate(
                [own, edge_tile(y_below, y_above, kind, c, z)], axis=0
            )
        return tall[kind, c, z]

    for index, plane in enumerate(DOWN_PLANES):
        down = whole(*plane)
        if plane == LABEL_PLANE:
            down = jnp.where(lane == WIDTH - 1, labels[SY : SY + 1, :], down)
        up = whole(*UP_PLANES[index]) if index < len(UP_PLANES) else down
        first[index] = jnp.where(even, up, down)
        second[index] = jnp.where(even, down, up)


def roll_x(value, shift):
    return pltpu.roll(value, shift % WIDTH, 1)


def roll_y(value, shift):
    return pltpu.roll(value, shift % TALL, 0)


class Planes:
    def __init__(self, mine, offset, given=None):
        self.mine, self.offset, self.given = mine, offset, given
        self.written = set()

    def where(self, lead, z, tile, ref, offset):
        rows = slice(None) if tile is None else slice(8 * tile, 8 * tile + 8)
        return ref, (*lead, z + offset, rows, slice(None))

    def load(self, *lead, z, tile=None):
        own = {(*lead, z, t) in self.written for t in (range(3) if tile is None else (tile,))}
        assert len(own) == 1
        if own.pop():
            ref, at = self.where(lead, z, tile, self.mine, self.offset)
        else:
            ref, at = self.where(lead, z, tile, self.given, 0)
        return ref[at]

    def store(self, value, *lead, z, tile=None):
        self.written |= {(*lead, z, t) for t in (range(3) if tile is None else (tile,))}
        ref, at = self.where(lead, z, tile, self.mine, self.offset)
        ref[at] = value


def fill(state, planes, own_block=None, z_part=None):
    work, loads, elem = state[:3]
    slab_pos, sub_pos = lax.axis_index("slab"), lax.axis_index("sub")
    last_slab, last_sub = lax.axis_size("slab") - 1, lax.axis_size("sub") - 1

    def gather(kind, c, z):
        if z < 0:
            return z_part[UP_PLANES.index((kind, c, z + DEPTH))]
        if z >= DEPTH:
            return z_part[DOWN_PLANES.index((kind, c, z - DEPTH))]
        field, load, modulus, y_below, y_above = own_block
        own = (field if kind == FIELD else load)[c, z] if kind != MODULUS else modulus[z]
        return jnp.concatenate([own, edge_tile(y_below, y_above, kind, c, z)], axis=0)

    row = lax.broadcasted_iota(jnp.int32, (TALL, WIDTH), 0)
    lane = lax.broadcasted_iota(jnp.int32, (TALL, WIDTH), 1)
    inside = (lane < WIDTH - 1) & ((row != ROWS - 1) | (sub_pos != last_sub))
    inside_top = inside & (slab_pos != last_slab)
    for z in planes:
        if -3 <= z <= 10:
            value = gather(MODULUS, 0, z)
            elem.store(jnp.where(inside_top if z == DEPTH - 1 else inside, value, 0.0), z=z)
        for c in range(3):
            work.store(gather(FIELD, c, z), c, z=z)
            if -2 <= z <= 10:
                loads.store(gather(LOAD, c, z), c, z=z)


def invert(state, first, last):
    elem, inv = state[2], state[3]
    diag_scale = (LAME + 4.0 * SHEAR) / 9.0
    off_scale = (LAME + SHEAR) / 12.0
    before = None
    for z in range(first - 1, last + 1):
        e = elem.load(z=z)
        right = roll_x(e, 1)
        sum_x, dif_x = e + right, right - e
        sum_up, dif_up = roll_y(sum_x, 1), roll_y(dif_x, 1)
        now = (sum_up + sum_x, sum_up - sum_x, dif_up + dif_x, dif_up - dif_x)
        if before is not None:
            p = diag_scale * (before[0] + now[0])
            cc = off_scale * (before[1] - now[1])
            b = off_scale * (before[2] - now[2])
            a = off_scale * (before[3] + now[3])
            pp = p * p
            co00, co11, co22 = pp - cc * cc, pp - b * b, pp - a * a
            co01, co02, co12 = b * cc - a * p, a * cc - b * p, a * b - p * cc
            det = p * co00 + a * co01 + b * co02
            scale = jnp.where(det != 0.0, DAMPING / det, 0.0)
            for k, value in enumerate((co00, co01, co02, co11, co12, co22)):
                inv.store(value * scale, k, z=z)
        before = now


def spread(state, planes):
    work, modes = state[0], state[4]
    for c in range(3):
        for z in planes:
            v = work.load(c, z=z)
            left = roll_x(v, -1)
            sum_x, dif_x = v + left, left - v
            sum_up, dif_up = roll_y(sum_x, -1), roll_y(dif_x, -1)
            modes.store(sum_x + sum_up, 4 * c, z=z)
            modes.store(dif_x + dif_up, 4 * c + 1, z=z)
            modes.store(sum_up - sum_x, 4 * c + 2, z=z)
            modes.store(dif_up - dif_x, 4 * c + 3, z=z)


def stress(state, lo, hi, resume=False, join=False):
    elem, modes, forces = state[2], state[4], state[5]
    for tile in range(3):
        old = [modes.load(k, z=lo, tile=tile) for k in range(12)]
        held = [forces.load(k, z=lo, tile=tile) for k in range(12)] if resume else None
        for z in range(lo, hi):
            e = elem.load(z=z, tile=tile)
            new = [modes.load(k, z=z + 1, tile=tile) for k in range(12)]
            total = [None if k % 4 == 0 else new[k] + old[k] for k in range(12)]
            delta = [new[k] - old[k] for k in range(12)]
            xa, xb, xc = total[1], total[2], total[3]
            xd, xe, xf, xg = delta[0], delta[1], delta[2], delta[3]
            ya, yb, yc = total[5], total[6], total[7]
            yd, ye, yf, yg = delta[4], delta[5], delta[6], delta[7]
            za, zb, zc = total[9], total[10], total[11]
            zd, ze, zf, zg = delta[8], delta[9], delta[10], delta[11]
            lam0, mu0 = e * (LAME / 16.0), e * (SHEAR / 16.0)
            lam1, mu1 = e * (LAME / 48.0), e * (SHEAR / 48.0)
            twice = e * (SHEAR / 8.0)
            last_scale = e * ((LAME + 4.0 * SHEAR) / 144.0)
            t = lam0 * (xa + yb + zd)
            xy, xz, yz = mu0 * (xb + ya), mu0 * (xd + za), mu0 * (yd + zb)
            s_x, s_y, s_z = lam1 * (yc + ze), lam1 * (xc + zf), lam1 * (xe + yf)
            q = xf + ye + zc
            even = (
                None, t + twice * xa, xy, s_y + mu0 * xc,
                None, xy, t + twice * yb, s_x + mu0 * yc,
                None, xz, yz, mu1 * (q + zc),
            )
            odd = (
                xz, s_z + mu0 * xe, mu1 * (q + xf), last_scale * xg,
                yz, mu1 * (q + ye), s_z + mu0 * yf, last_scale * yg,
                t + twice * zd, s_x + mu0 * ze, s_y + mu0 * zf, last_scale * zg,
            )
            for k in range(12):
                low = -odd[k] if even[k] is None else even[k] - odd[k]
                forces.store(low if held is None else held[k] + low, k, z=z, tile=tile)
            held = [odd[k] if even[k] is None else even[k] + odd[k] for k in range(12)]
            old = new
        for k in range(12):
            total = forces.load(k, z=hi, tile=tile) + held[k] if join else held[k]
            forces.store(total, k, z=hi, tile=tile)


def misfit(state, z):
    loads, forces = state[1], state[5]
    out = []
    for c in range(3):
        f = [forces.load(4 * c + k, z=z) for k in range(4)]
        sum_x = (f[0] - f[2]) + roll_y(f[0] + f[2], 1)
        dif_x = (f[1] - f[3]) + roll_y(f[1] + f[3], 1)
        out.append(loads.load(c, z=z) - ((sum_x - dif_x) + roll_x(sum_x + dif_x, 1)))
    return out


def relax(state, planes):
    work, inv = state[0], state[3]
    table = ((0, 1, 2), (1, 3, 4), (2, 4, 5))
    for z in planes:
        m = [inv.load(k, z=z) for k in range(6)]
        r = misfit(state, z)
        for c in range(3):
            i, j, k = table[c]
            step = m[i] * r[0] + m[j] * r[1] + m[k] * r[2]
            work.store(work.load(c, z=z) + step, c, z=z)


def solve_inner(even, *refs):
    @pl.when(is_even("slab") == even)
    def mine():
        inner(*refs)


def inner(field, load, modulus, y_below, y_above, *refs):
    state = [Planes(ref, 0) for ref in refs[:6]]
    residual = refs[6]
    fill(state, range(0, 8), own_block=(field, load, modulus, y_below, y_above))
    invert(state, 1, 7)
    spread(state, range(0, 8))
    stress(state, 0, 7)
    relax(state, range(1, 7))
    spread(state, range(1, 7))
    stress(state, 1, 6)
    relax(state, range(2, 6))
    spread(state, range(2, 6))
    stress(state, 2, 5)
    for z in (3, 4):
        for c, value in enumerate(misfit(state, z)):
            residual[c, z - 3] = value


LOWER, UPPER = (0, 1), (6, 7)


def solve_side(lower, z_part, given, mine, smooth, smooth_from):
    state = [Planes(ref, 3, old) for ref, old in zip(mine, given)]
    if lower:
        fill(state, range(-3, 0), z_part=z_part)
        invert(state, -2, 0)
        for first, last in ((-3, 0), (-2, 1), (-1, 2)):
            spread(state, range(first, last))
            stress(state, first, last, join=True)
            if last < 2:
                relax(state, range(first + 1, last + 1))
    else:
        fill(state, range(8, 12), z_part=z_part)
        invert(state, 8, 10)
        for first, last in ((7, 11), (6, 10), (5, 9)):
            spread(state, range(first + 1, last + 1))
            stress(state, first, last, resume=True)
            if last > 9:
                relax(state, range(first, last))
    for k, z in enumerate(LOWER if lower else UPPER):
        for c in range(3):
            smooth[c, smooth_from + k] = state[0].load(c, z=z)[:ROWS]
    return {z: misfit(state, z) for z in ((0, 1, 2) if lower else (5, 6, 7, 8))}


def prepare(labels, chosen):
    target = lax.broadcasted_iota(jnp.int32, (WIDTH, WIDTH), 0) % SX
    hit = jnp.where(target.astype(jnp.float32) == labels[7:8, :], 1.0, 0.0)
    chosen[...] = hit.astype(jnp.bfloat16)


def restrict(kz, residual, labels, chosen, y_label, z_label, rows):
    slab_pos, sub_pos = lax.axis_index("slab"), lax.axis_index("sub")
    last_slab, last_sub = lax.axis_size("slab") - 1, lax.axis_size("sub") - 1
    row = lax.broadcasted_iota(jnp.int32, (TALL, WIDTH), 0)

    def flag(value, segment):
        return jnp.where(value == segment.astype(jnp.float32), 1.0, 0.0)

    start_z = SZ * slab_pos + kz
    low = flag(labels[SY + kz : SY + kz + 1, :], start_z)
    if kz == 0:
        high = flag(labels[SY + 1 : SY + 2, :], start_z)
    else:
        high = jnp.where(slab_pos != last_slab, flag(z_label, start_z), 0.0)
    sums = [None] * 5
    for step in range(5):
        r = residual[4 * kz + step]
        if step in (0, 4):
            r = [(low if step == 0 else high) * value for value in r]
        q = 0.5 * (step - 2)
        terms = [r[0], r[1], r[2], q * r[1], q * r[0]]
        for k in range(5 if q != 0.0 else 3):
            sums[k] = terms[k] if sums[k] is None else sums[k] + terms[k]
    r0, r1, r2, z1, z0 = sums
    count_z, moment_z = low + 3.0 + high, high - low

    start_y = SY * sub_pos
    owns_next = jnp.where(sub_pos != last_sub, flag(y_label, start_y + SY - 1), 0.0)
    lane = lax.broadcasted_iota(jnp.int32, (1, WIDTH), 1)
    group = lane // SX
    seg_x = labels[7:8, :]
    q_x = 0.5 * (lane.astype(jnp.float32) - 4.0 * seg_x - 2.0)
    count_y = jnp.zeros((1, WIDTH), jnp.float32)
    moment_y = jnp.zeros((1, WIDTH), jnp.float32)

    def total(value):
        return jnp.sum(value, axis=0, keepdims=True)

    for ky in range(SY):
        first = flag(labels[ky : ky + 1, :], start_y + ky)
        final = flag(labels[ky + 1 : ky + 2, :], start_y + ky) if ky < SY - 1 else owns_next
        local = row - 4 * ky
        weight = jnp.where((local > 0) & (local < 4), 1.0, 0.0)
        weight = jnp.where(local == 0, first, jnp.where(local == 4, final, weight))
        moment = weight * (0.5 * (local - 2).astype(jnp.float32))
        count_y = jnp.where(group == ky, first + 3.0 + final, count_y)
        moment_y = jnp.where(group == ky, final - first, moment_y)
        plain = [total(weight * value) for value in (r0, r1, r2)]
        turned = [
            total(moment * r2 - weight * z1),
            total(weight * z0) - q_x * plain[2],
            q_x * plain[1] - total(moment * r0),
        ]
        for k, value in enumerate(plain + turned + [jnp.ones((1, WIDTH), jnp.float32), q_x]):
            rows[8 * ky + k : 8 * ky + k + 1, :] = value

    rest, parts = rows[...], []
    for _ in range(3):
        parts.append(rest.astype(jnp.bfloat16))
        rest = rest - parts[-1].astype(jnp.float32)
    totals = lax.dot_general(
        jnp.concatenate(parts, axis=0), chosen[...], (((1,), (1,)), ((), ())),
        preferred_element_type=jnp.float32,
    )
    totals = totals[0:32] + totals[32:64] + totals[64:96]
    s = totals[0:8]
    for ky in range(1, SY):
        s = jnp.where(group == ky, totals[8 * ky : 8 * ky + 8], s)
    s = [s[k : k + 1] for k in range(8)]
    count_x, moment_x = s[6], s[7]
    count = count_x * count_y * count_z
    centre = [
        moment_x * count_y * count_z / count,
        count_x * moment_y * count_z / count,
        count_x * count_y * moment_z / count,
    ]
    scale = 1.0 / jnp.sqrt(count)
    turned = [
        s[3] - (centre[1] * s[2] - centre[2] * s[1]),
        s[4] - (centre[2] * s[0] - centre[0] * s[2]),
        s[5] - (centre[0] * s[1] - centre[1] * s[0]),
    ]
    return [value * scale for value in s[:3] + turned]


def z_label(part):
    row = part[DOWN_PLANES.index(LABEL_PLANE), 0:1, :]
    return jnp.broadcast_to(row[:, WIDTH - 1 :], (1, WIDTH))


def with_middle(residual, middle):
    residual |= {z: [middle[c, z - 3] for c in range(3)] for z in (3, 4)}
    return residual


def solve_near(labels, chosen, y_above, z_first, *refs):
    states, (smooth, coarse), rows, mine = (refs[7:14], refs[:7]), refs[14:16], refs[16], refs[17:23]
    for lower in (False, True):
        *given, middle = states[lower]

        @pl.when(is_even("slab") != lower)
        def side(given=given, middle=middle):
            residual = solve_side(lower, z_first, given, mine, smooth, 0)
            coarse_rows = restrict(
                0 if lower else 1, with_middle(residual, middle), labels, chosen,
                y_above[DOWN_SIZE : DOWN_SIZE + 1, :], z_label(z_first), rows,
            )
            for k in range(6):
                coarse[k : k + 1, :] = coarse_rows[k]


def solve_far(labels, chosen, y_above, z_second, *refs):
    states, (near_smooth, near_coarse) = (refs[:7], refs[7:14]), refs[14:16]
    (smooth, coarse), rows, mine = refs[16:18], refs[18], refs[19:25]

    for lower in (True, False):
        *given, middle = states[lower]

        @pl.when(is_even("slab") == lower)
        def side(given=given, middle=middle):
            near, far, kz = (UPPER, LOWER, 0) if lower else (LOWER, UPPER, 1)
            for c in range(3):
                for z in range(2, 6):
                    smooth[c, z] = given[0][c, z, :ROWS, :]
                for k, z in enumerate(near):
                    smooth[c, z] = near_smooth[c, k]
            residual = solve_side(lower, z_second, given, mine, smooth, far[0])
            coarse_rows = restrict(
                kz, with_middle(residual, middle), labels, chosen,
                y_above[DOWN_SIZE : DOWN_SIZE + 1, :], z_label(z_second), rows,
            )
            for k in range(6):
                coarse[k, kz : kz + 1, :] = coarse_rows[k]
                coarse[k, 1 - kz : 2 - kz, :] = near_coarse[k : k + 1, :]


VMEM = pl.BlockSpec(memory_space=pltpu.VMEM)


def f32(*shape):
    return jax.ShapeDtypeStruct(shape, jnp.float32)


def scratch(*shape):
    return pltpu.VMEM(shape, jnp.float32)


def on_device(field_init, load, modulus, seg_z, seg_y, seg_x):
    def swap(block, axis, start):
        pairs = [(i, i + 1) for i in range(start, lax.axis_size(axis) - 1, 2)]
        return lax.ppermute(block, axis, pairs + [(j, i) for i, j in pairs])

    def limit(mib):
        return pltpu.CompilerParams(vmem_limit_bytes=mib << 20)

    hbm = pl.BlockSpec(memory_space=pltpu.MemorySpace.HBM)
    blocks = [f32(3, DEPTH, ROWS, WIDTH), f32(3, DEPTH, ROWS, WIDTH), f32(DEPTH, ROWS, WIDTH)]
    arguments = (seg_y, seg_z, seg_x, field_init, load, modulus)
    up, down, field_init, load, modulus, labels = pl.pallas_call(
        pack_y,
        out_shape=[f32(UP_SIZE, WIDTH), f32(DOWN_SIZE + 8, WIDTH)] + blocks + [f32(8, WIDTH)],
        in_specs=[hbm] * 6,
        out_specs=[VMEM] * 6,
        scratch_shapes=[
            pltpu.SMEM((ROWS,), jnp.int32),
            pltpu.SMEM((DEPTH,), jnp.int32),
            pltpu.VMEM((WIDTH,), jnp.int32),
            pltpu.SemaphoreType.DMA((6,)),
        ],
        compiler_params=limit(4),
        name="pack_y",
    )(*[pltpu.with_memory_space_constraint(value, pltpu.MemorySpace.HBM) for value in arguments])
    steps = [(i, i + 1) for i in range(lax.axis_size("sub") - 1)]
    y_above = lax.ppermute(down, "sub", [(j, i) for i, j in steps])
    y_below = lax.ppermute(up, "sub", steps)
    y_parts = (y_below, y_above)
    chosen = pl.pallas_call(
        prepare,
        out_shape=jax.ShapeDtypeStruct((WIDTH, WIDTH), jnp.bfloat16),
        in_specs=[VMEM],
        out_specs=VMEM,
        compiler_params=limit(1),
        name="prepare",
    )(labels)
    first, second = pl.pallas_call(
        pack_z,
        out_shape=(f32(len(DOWN_PLANES), TALL, WIDTH),) * 2,
        in_specs=[VMEM] * 6,
        out_specs=(VMEM, VMEM),
        compiler_params=limit(4),
        name="pack_z",
    )(labels, field_init, load, modulus, *y_parts)
    z_second = swap(second, "slab", 1)
    z_first = swap(first, "slab", 0)

    def sizes(planes):
        return [(3, planes, TALL, WIDTH)] * 2 + [(planes, TALL, WIDTH)] + [
            (n, planes, TALL, WIDTH) for n in (6, 12, 12)
        ]

    states = []
    for even in (False, True):
        states += pl.pallas_call(
            functools.partial(solve_inner, even),
            out_shape=[f32(*size) for size in sizes(DEPTH)] + [f32(3, 2, TALL, WIDTH)],
            in_specs=[VMEM] * 5,
            out_specs=[VMEM] * 7,
            compiler_params=limit(6),
        )(field_init, load, modulus, *y_parts)
    near = pl.pallas_call(
        solve_near,
        out_shape=(f32(3, 2, ROWS, WIDTH), f32(8, WIDTH)),
        in_specs=[VMEM] * 18,
        out_specs=(VMEM, VMEM),
        scratch_shapes=[scratch(8 * SY, WIDTH)] + [scratch(*size) for size in sizes(15)],
        compiler_params=limit(12),
        name="solve_near",
    )(labels, chosen, y_above, z_first, *states)
    return pl.pallas_call(
        solve_far,
        out_shape=(f32(3, DEPTH, ROWS, WIDTH), f32(6, SZ, SY * SX)),
        in_specs=[VMEM] * 20,
        out_specs=(VMEM, VMEM),
        scratch_shapes=[scratch(8 * SY, WIDTH)] + [scratch(*size) for size in sizes(15)],
        compiler_params=limit(14),
        name="solve_far",
    )(labels, chosen, y_above, z_second, *states, *near)


def solution(mesh):
    in_specs = (
        P(None, "slab", "sub", None),
        P(None, "slab", "sub", None),
        P("slab", "sub", None),
        P("slab"),
        P("sub"),
        P(),
    )
    out_specs = (P(None, "slab", "sub", None), P(None, "slab", "sub"))
    return jax.shard_map(
        on_device, mesh=mesh, in_specs=in_specs, out_specs=out_specs, check_vma=False
    )
```

```python
import functools

import jax
import jax.numpy as jnp
from jax import lax
from jax.experimental import pallas as pl
from jax.experimental.pallas import tpu as pltpu
from jax.sharding import PartitionSpec as P


SX = 32
SY = 4
SZ = 2
DEPTH = 8
ROWS = 16
WIDTH = 128
TALL = 24
DAMPING = 0.6

POISSON = 0.3
LAME = POISSON / ((1.0 + POISSON) * (1.0 - 2.0 * POISSON))
SHEAR = 0.5 / (1.0 + POISSON)

FIELD, LOAD, MODULUS = 0, 1, 2
UP_ROWS, DOWN_ROWS = (3, 2, 3), (4, 3, 3)
UP_AT, DOWN_AT = (0, 72, 120), (0, 96, 168)
DOWN_SIZE = 192
UP_PLANES = (
    [(FIELD, c, z) for c in range(3) for z in (5, 6, 7)]
    + [(LOAD, c, z) for c in range(3) for z in (6, 7)]
    + [(MODULUS, 0, z) for z in (5, 6, 7)]
)
DOWN_PLANES = (
    [(FIELD, c, z) for c in range(3) for z in (0, 1, 2, 3)]
    + [(LOAD, c, z) for c in range(3) for z in (0, 1, 2)]
    + [(MODULUS, 0, z) for z in (0, 1, 2)]
)


LABEL_PLANE = (MODULUS, 0, 0)


def y_rows(kind, c, z, up):
    rows, start = (UP_ROWS[kind], UP_AT[kind]) if up else (DOWN_ROWS[kind], DOWN_AT[kind])
    start += rows * (DEPTH * c + z)
    return slice(start, start + rows)


def is_even(axis):
    return lax.axis_index(axis) % 2 == 0


def pack_y(
    seg_y_hbm, seg_z_hbm, seg_x_hbm, field_hbm, load_hbm, modulus_hbm,
    first, second, field, load, modulus, labels, up, down, seg_y, seg_z, seg_x, sems,
):
    pairs = [(field_hbm.at[c], field.at[c]) for c in range(3)]
    pairs += [(load_hbm.at[c], load.at[c]) for c in range(3)]
    pairs += [
        (modulus_hbm, modulus), (seg_y_hbm, seg_y), (seg_z_hbm, seg_z), (seg_x_hbm, seg_x),
    ]
    copies = [pltpu.make_async_copy(src, dst, sems.at[k]) for k, (src, dst) in enumerate(pairs)]
    for copy in copies:
        copy.start()
    for ref, kind in ((field, FIELD), (load, LOAD), (modulus, MODULUS)):
        for c in range(1 if kind == MODULUS else 3):
            copies[3 * kind + c].wait()
            for z in range(DEPTH):
                at = (z,) if kind == MODULUS else (c, z)
                up[y_rows(kind, c, z, True), :] = ref[(*at, slice(ROWS - UP_ROWS[kind], ROWS), slice(None))]
                down[y_rows(kind, c, z, False), :] = ref[(*at, slice(0, DOWN_ROWS[kind]), slice(None))]
    for copy in copies[7:]:
        copy.wait()
    down[DOWN_SIZE:, :] = jnp.full((8, WIDTH), seg_y[0].astype(jnp.float32))
    upward = (lax.axis_index("slab") == 0) & is_even("sub")
    first[...] = jnp.where(upward, up[...], down[...])
    second[...] = jnp.where(upward, down[...], up[...])
    for k in range(SY):
        labels[k : k + 1, :] = jnp.full((1, WIDTH), seg_y[4 * k].astype(jnp.float32))
    for k in range(SZ):
        labels[SY + k : SY + k + 1, :] = jnp.full((1, WIDTH), seg_z[4 * k].astype(jnp.float32))
    labels[7:8, :] = seg_x[...].reshape(1, WIDTH).astype(jnp.float32)


def edge_tile(below, above, kind, c, z):
    parts = [above[y_rows(kind, c, z, False), :]]
    spare = 8 - UP_ROWS[kind] - DOWN_ROWS[kind]
    parts.append(jnp.zeros((spare, WIDTH), jnp.float32))
    parts.append(below[y_rows(kind, c, z, True), :])
    return jnp.concatenate(parts, axis=0)


def pack_z(labels, field, load, modulus, y_first, y_second, first, second, y_below, y_above):
    below_first = (lax.axis_index("slab") == 0) & jnp.logical_not(is_even("sub"))
    y_below[...] = jnp.where(below_first, y_first[...], y_second[...])
    y_above[...] = jnp.where(below_first, y_second[...], y_first[...])
    even = is_even("slab")
    lane = lax.broadcasted_iota(jnp.int32, (TALL, WIDTH), 1)
    tall = {}

    def whole(kind, c, z):
        if (kind, c, z) not in tall:
            own = (field if kind == FIELD else load)[c, z] if kind != MODULUS else modulus[z]
            tall[kind, c, z] = jnp.concatenate(
                [own, edge_tile(y_below, y_above, kind, c, z)], axis=0
            )
        return tall[kind, c, z]

    for index, plane in enumerate(DOWN_PLANES):
        down = whole(*plane)
        if plane == LABEL_PLANE:
            down = jnp.where(lane == WIDTH - 1, labels[SY : SY + 1, :], down)
        up = whole(*UP_PLANES[index]) if index < len(UP_PLANES) else down
        first[index] = jnp.where(even, up, down)
        second[index] = jnp.where(even, down, up)


def roll_x(value, shift):
    return pltpu.roll(value, shift % WIDTH, 1)


def roll_y(value, shift):
    return pltpu.roll(value, shift % TALL, 0)


class Planes:
    def __init__(self, mine, offset, given=None):
        self.mine, self.offset, self.given = mine, offset, given
        self.written = set()

    def where(self, lead, z, tile, ref, offset):
        rows = slice(None) if tile is None else slice(8 * tile, 8 * tile + 8)
        return ref, (*lead, z + offset, rows, slice(None))

    def load(self, *lead, z, tile=None):
        own = {(*lead, z, t) in self.written for t in (range(3) if tile is None else (tile,))}
        assert len(own) == 1
        if own.pop():
            ref, at = self.where(lead, z, tile, self.mine, self.offset)
        else:
            ref, at = self.where(lead, z, tile, self.given, 0)
        return ref[at]

    def store(self, value, *lead, z, tile=None):
        self.written |= {(*lead, z, t) for t in (range(3) if tile is None else (tile,))}
        ref, at = self.where(lead, z, tile, self.mine, self.offset)
        ref[at] = value


def fill(state, planes, own_block=None, z_part=None):
    work, loads, elem = state[:3]
    slab_pos, sub_pos = lax.axis_index("slab"), lax.axis_index("sub")
    last_slab, last_sub = lax.axis_size("slab") - 1, lax.axis_size("sub") - 1

    def gather(kind, c, z):
        if z < 0:
            return z_part[UP_PLANES.index((kind, c, z + DEPTH))]
        if z >= DEPTH:
            return z_part[DOWN_PLANES.index((kind, c, z - DEPTH))]
        field, load, modulus, y_below, y_above = own_block
        own = (field if kind == FIELD else load)[c, z] if kind != MODULUS else modulus[z]
        return jnp.concatenate([own, edge_tile(y_below, y_above, kind, c, z)], axis=0)

    row = lax.broadcasted_iota(jnp.int32, (TALL, WIDTH), 0)
    lane = lax.broadcasted_iota(jnp.int32, (TALL, WIDTH), 1)
    inside = (lane < WIDTH - 1) & ((row != ROWS - 1) | (sub_pos != last_sub))
    inside_top = inside & (slab_pos != last_slab)
    for z in planes:
        if -3 <= z <= 10:
            value = gather(MODULUS, 0, z)
            elem.store(jnp.where(inside_top if z == DEPTH - 1 else inside, value, 0.0), z=z)
        for c in range(3):
            work.store(gather(FIELD, c, z), c, z=z)
            if -2 <= z <= 10:
                loads.store(gather(LOAD, c, z), c, z=z)


def invert(state, first, last):
    elem, inv = state[2], state[3]
    diag_scale = (LAME + 4.0 * SHEAR) / 9.0
    off_scale = (LAME + SHEAR) / 12.0
    before = None
    for z in range(first - 1, last + 1):
        e = elem.load(z=z)
        up = roll_y(e, 1)
        sum_y, dif_y = e + up, up - e
        sum_right, dif_right = roll_x(sum_y, 1), roll_x(dif_y, 1)
        now = (sum_y + sum_right, dif_y + dif_right, sum_right - sum_y, dif_right - dif_y)
        if before is not None:
            p = (diag_scale / off_scale) * (before[0] + now[0])
            cc = before[1] - now[1]
            b = before[2] - now[2]
            a = before[3] + now[3]
            pp = p * p
            co00, co11, co22 = pp - cc * cc, pp - b * b, pp - a * a
            co01, co02, co12 = b * cc - a * p, a * cc - b * p, a * b - p * cc
            det = p * co00 + a * co01 + b * co02
            scale = jnp.where(det != 0.0, (DAMPING / off_scale) / det, 0.0)
            for k, value in enumerate((co00, co01, co02, co11, co12, co22)):
                inv.store(value * scale, k, z=z)
        before = now


def spread(state, planes):
    work, modes = state[0], state[4]
    for c in range(3):
        for z in planes:
            v = work.load(c, z=z)
            up = roll_y(v, -1)
            sum_y, dif_y = v + up, up - v
            sum_left, dif_left = roll_x(sum_y, -1), roll_x(dif_y, -1)
            modes.store(sum_y + sum_left, 4 * c, z=z)
            modes.store(sum_left - sum_y, 4 * c + 1, z=z)
            modes.store(dif_y + dif_left, 4 * c + 2, z=z)
            modes.store(dif_left - dif_y, 4 * c + 3, z=z)


def stress(state, lo, hi, resume=False, join=False):
    elem, modes, forces = state[2], state[4], state[5]
    for tile in range(3):
        old = [modes.load(k, z=lo, tile=tile) for k in range(12)]
        held = [forces.load(k, z=lo, tile=tile) for k in range(12)] if resume else None
        for z in range(lo, hi):
            e = elem.load(z=z, tile=tile)
            new = [modes.load(k, z=z + 1, tile=tile) for k in range(12)]
            total = [None if k % 4 == 0 else new[k] + old[k] for k in range(12)]
            delta = [new[k] - old[k] for k in range(12)]
            xa, xb, xc = total[1], total[2], total[3]
            xd, xe, xf, xg = delta[0], delta[1], delta[2], delta[3]
            ya, yb, yc = total[5], total[6], total[7]
            yd, ye, yf, yg = delta[4], delta[5], delta[6], delta[7]
            za, zb, zc = total[9], total[10], total[11]
            zd, ze, zf, zg = delta[8], delta[9], delta[10], delta[11]
            lam0, mu0 = e * (LAME / 16.0), e * (SHEAR / 16.0)
            lam1, mu1 = e * (LAME / 48.0), e * (SHEAR / 48.0)
            twice = e * (SHEAR / 8.0)
            last_scale = e * ((LAME + 4.0 * SHEAR) / 144.0)
            t = lam0 * (xa + yb + zd)
            xy, xz, yz = mu0 * (xb + ya), mu0 * (xd + za), mu0 * (yd + zb)
            s_x, s_y, s_z = lam1 * (yc + ze), lam1 * (xc + zf), lam1 * (xe + yf)
            q = xf + ye + zc
            even = (
                None, t + twice * xa, xy, s_y + mu0 * xc,
                None, xy, t + twice * yb, s_x + mu0 * yc,
                None, xz, yz, mu1 * (q + zc),
            )
            odd = (
                xz, s_z + mu0 * xe, mu1 * (q + xf), last_scale * xg,
                yz, mu1 * (q + ye), s_z + mu0 * yf, last_scale * yg,
                t + twice * zd, s_x + mu0 * ze, s_y + mu0 * zf, last_scale * zg,
            )
            for k in range(12):
                if even[k] is None:
                    low = -odd[k] if held is None else held[k] - odd[k]
                else:
                    low = even[k] - odd[k] if held is None else held[k] + (even[k] - odd[k])
                forces.store(low, k, z=z, tile=tile)
            held = [odd[k] if even[k] is None else even[k] + odd[k] for k in range(12)]
            old = new
        for k in range(12):
            total = forces.load(k, z=hi, tile=tile) + held[k] if join else held[k]
            forces.store(total, k, z=hi, tile=tile)


def misfit(state, z):
    loads, forces = state[1], state[5]
    out = []
    for c in range(3):
        f = [forces.load(4 * c + k, z=z) for k in range(4)]
        sum_y = (f[0] - f[1]) + roll_x(f[0] + f[1], 1)
        dif_y = (f[2] - f[3]) + roll_x(f[2] + f[3], 1)
        out.append(loads.load(c, z=z) - ((sum_y - dif_y) + roll_y(sum_y + dif_y, 1)))
    return out


def relax(state, planes):
    work, inv = state[0], state[3]
    table = ((0, 1, 2), (1, 3, 4), (2, 4, 5))
    for z in planes:
        m = [inv.load(k, z=z) for k in range(6)]
        r = misfit(state, z)
        for c in range(3):
            i, j, k = table[c]
            step = m[i] * r[0] + m[j] * r[1] + m[k] * r[2]
            work.store(work.load(c, z=z) + step, c, z=z)


def solve_inner(even, *refs):
    @pl.when(is_even("slab") == even)
    def mine():
        inner(*refs)


def inner(field, load, modulus, y_below, y_above, *refs):
    state = [Planes(ref, 0) for ref in refs[:6]]
    residual = refs[6]
    fill(state, range(0, 8), own_block=(field, load, modulus, y_below, y_above))
    invert(state, 1, 7)
    spread(state, range(0, 8))
    stress(state, 0, 7)
    relax(state, range(1, 7))
    spread(state, range(1, 7))
    stress(state, 1, 6)
    relax(state, range(2, 6))
    spread(state, range(2, 6))
    stress(state, 2, 5)
    for z in (3, 4):
        for c, value in enumerate(misfit(state, z)):
            residual[c, z - 3] = value


LOWER, UPPER = (0, 1), (6, 7)


def solve_side(lower, z_part, given, mine, smoothed):
    state = [Planes(ref, 3, old) for ref, old in zip(mine, given)]
    if lower:
        fill(state, range(-3, 0), z_part=z_part)
        invert(state, -2, 0)
        rounds = ((-3, 0), (-2, 1), (-1, 2))
    else:
        fill(state, range(8, 12), z_part=z_part)
        invert(state, 8, 10)
        rounds = ((7, 11), (6, 10), (5, 9))
    for step, (first, last) in enumerate(rounds):
        spread(state, range(first, last) if lower else range(first + 1, last + 1))
        stress(state, first, last, join=lower, resume=not lower)
        if step < 2:
            relax(state, range(first + 1, last + 1) if lower else range(first, last))
        if step == 1:
            smoothed()
    return {z: misfit(state, z) for z in ((0, 1, 2) if lower else (5, 6, 7, 8))}


def prepare(labels, chosen):
    target = lax.broadcasted_iota(jnp.int32, (WIDTH, WIDTH), 0) % SX
    hit = jnp.where(target.astype(jnp.float32) == labels[7:8, :], 1.0, 0.0)
    chosen[...] = hit.astype(jnp.bfloat16)


def restrict(kz, residual, labels, chosen, y_label, z_label, rows):
    slab_pos, sub_pos = lax.axis_index("slab"), lax.axis_index("sub")
    last_slab, last_sub = lax.axis_size("slab") - 1, lax.axis_size("sub") - 1
    row = lax.broadcasted_iota(jnp.int32, (TALL, WIDTH), 0)

    def flag(value, segment):
        return jnp.where(value == segment.astype(jnp.float32), 1.0, 0.0)

    start_z = SZ * slab_pos + kz
    low = flag(labels[SY + kz : SY + kz + 1, :], start_z)
    if kz == 0:
        high = flag(labels[SY + 1 : SY + 2, :], start_z)
    else:
        high = jnp.where(slab_pos != last_slab, flag(z_label, start_z), 0.0)
    sums = [None] * 5
    for step in range(5):
        r = residual[4 * kz + step]
        if step in (0, 4):
            r = [(low if step == 0 else high) * value for value in r]
        q = 0.5 * (step - 2)
        terms = [r[0], r[1], r[2], q * r[1], q * r[0]]
        for k in range(5 if q != 0.0 else 3):
            sums[k] = terms[k] if sums[k] is None else sums[k] + terms[k]
    r0, r1, r2, z1, z0 = sums
    count_z, moment_z = low + 3.0 + high, high - low

    start_y = SY * sub_pos
    owns_next = jnp.where(sub_pos != last_sub, flag(y_label, start_y + SY - 1), 0.0)
    lane = lax.broadcasted_iota(jnp.int32, (1, WIDTH), 1)
    group = lane // SX
    seg_x = labels[7:8, :]
    q_x = 0.5 * (lane.astype(jnp.float32) - 4.0 * seg_x - 2.0)
    count_y = jnp.zeros((1, WIDTH), jnp.float32)
    moment_y = jnp.zeros((1, WIDTH), jnp.float32)

    def total(value):
        return jnp.sum(value, axis=0, keepdims=True)

    for ky in range(SY):
        first = flag(labels[ky : ky + 1, :], start_y + ky)
        final = flag(labels[ky + 1 : ky + 2, :], start_y + ky) if ky < SY - 1 else owns_next
        local = row - 4 * ky
        weight = jnp.where((local > 0) & (local < 4), 1.0, 0.0)
        weight = jnp.where(local == 0, first, jnp.where(local == 4, final, weight))
        moment = weight * (0.5 * (local - 2).astype(jnp.float32))
        count_y = jnp.where(group == ky, first + 3.0 + final, count_y)
        moment_y = jnp.where(group == ky, final - first, moment_y)
        plain = [total(weight * value) for value in (r0, r1, r2)]
        turned = [
            total(moment * r2 - weight * z1),
            total(weight * z0) - q_x * plain[2],
            q_x * plain[1] - total(moment * r0),
        ]
        for k, value in enumerate(plain + turned + [jnp.ones((1, WIDTH), jnp.float32), q_x]):
            rows[8 * ky + k : 8 * ky + k + 1, :] = value

    rest, parts = rows[...], []
    for _ in range(3):
        parts.append(rest.astype(jnp.bfloat16))
        rest = rest - parts[-1].astype(jnp.float32)
    totals = lax.dot_general(
        jnp.concatenate(parts, axis=0), chosen[...], (((1,), (1,)), ((), ())),
        preferred_element_type=jnp.float32,
    )
    totals = totals[0:32] + totals[32:64] + totals[64:96]
    s = totals[0:8]
    for ky in range(1, SY):
        s = jnp.where(group == ky, totals[8 * ky : 8 * ky + 8], s)
    s = [s[k : k + 1] for k in range(8)]
    count_x, moment_x = s[6], s[7]
    count = count_x * count_y * count_z
    centre = [
        moment_x * count_y * count_z / count,
        count_x * moment_y * count_z / count,
        count_x * count_y * moment_z / count,
    ]
    scale = 1.0 / jnp.sqrt(count)
    turned = [
        s[3] - (centre[1] * s[2] - centre[2] * s[1]),
        s[4] - (centre[2] * s[0] - centre[0] * s[2]),
        s[5] - (centre[0] * s[1] - centre[1] * s[0]),
    ]
    return [value * scale for value in s[:3] + turned]


def z_label(part):
    row = part[DOWN_PLANES.index(LABEL_PLANE), 0:1, :]
    return jnp.broadcast_to(row[:, WIDTH - 1 :], (1, WIDTH))


def with_middle(residual, middle):
    residual |= {z: [middle[c, z - 3] for c in range(3)] for z in (3, 4)}
    return residual


def solve_near(labels, chosen, y_above, z_first, *refs):
    states, (smooth, coarse), rows, mine = (refs[7:14], refs[:7]), refs[14:16], refs[16], refs[17:23]
    for lower in (False, True):
        *given, middle = states[lower]

        @pl.when(is_even("slab") != lower)
        def side(given=given, middle=middle):
            def smoothed():
                for k, z in enumerate(LOWER if lower else UPPER):
                    for c in range(3):
                        smooth[c, k] = mine[0][c, z + 3, :ROWS, :]

            residual = solve_side(lower, z_first, given, mine, smoothed)
            coarse_rows = restrict(
                0 if lower else 1, with_middle(residual, middle), labels, chosen,
                y_above[DOWN_SIZE : DOWN_SIZE + 1, :], z_label(z_first), rows,
            )
            for k in range(6):
                coarse[k : k + 1, :] = coarse_rows[k]


def solve_far(labels, chosen, y_above, z_second, *refs):
    states, (near_smooth, near_coarse) = (refs[:7], refs[7:14]), refs[14:16]
    (smooth, coarse), rows, mine, sems = refs[16:18], refs[18], refs[19:25], refs[25]

    for lower in (True, False):
        *given, middle = states[lower]

        @pl.when(is_even("slab") == lower)
        def side(given=given, middle=middle):
            near, far, kz = (UPPER, LOWER, 0) if lower else (LOWER, UPPER, 1)
            planes = slice(far[0] + 3, far[1] + 4)
            copies = [
                pltpu.make_async_copy(src, smooth.at[:, out], sems.at[k])
                for k, (src, out) in enumerate((
                    (given[0].at[:, 2:6, :ROWS, :], slice(2, 6)),
                    (near_smooth, slice(near[0], near[1] + 1)),
                    (mine[0].at[:, planes, :ROWS, :], slice(far[0], far[1] + 1)),
                ))
            ]
            copies[0].start()
            copies[1].start()
            residual = solve_side(lower, z_second, given, mine, copies[2].start)
            coarse_rows = restrict(
                kz, with_middle(residual, middle), labels, chosen,
                y_above[DOWN_SIZE : DOWN_SIZE + 1, :], z_label(z_second), rows,
            )
            for k in range(6):
                coarse[k, kz : kz + 1, :] = coarse_rows[k]
                coarse[k, 1 - kz : 2 - kz, :] = near_coarse[k : k + 1, :]
            for copy in copies:
                copy.wait()


VMEM = pl.BlockSpec(memory_space=pltpu.VMEM)


def f32(*shape):
    return jax.ShapeDtypeStruct(shape, jnp.float32)


def scratch(*shape):
    return pltpu.VMEM(shape, jnp.float32)


def on_device(field_init, load, modulus, seg_z, seg_y, seg_x):
    def swap(block, axis, start):
        pairs = [(i, i + 1) for i in range(start, lax.axis_size(axis) - 1, 2)]
        return lax.ppermute(block, axis, pairs + [(j, i) for i, j in pairs])

    def limit(mib):
        return pltpu.CompilerParams(vmem_limit_bytes=mib << 20)

    hbm = pl.BlockSpec(memory_space=pltpu.MemorySpace.HBM)
    blocks = [f32(3, DEPTH, ROWS, WIDTH), f32(3, DEPTH, ROWS, WIDTH), f32(DEPTH, ROWS, WIDTH)]
    arguments = (seg_y, seg_z, seg_x, field_init, load, modulus)
    first, second, field_init, load, modulus, labels = pl.pallas_call(
        pack_y,
        out_shape=[f32(DOWN_SIZE + 8, WIDTH), f32(DOWN_SIZE + 8, WIDTH)] + blocks + [f32(8, WIDTH)],
        in_specs=[hbm] * 6,
        out_specs=[VMEM] * 6,
        scratch_shapes=[
            scratch(DOWN_SIZE + 8, WIDTH),
            scratch(DOWN_SIZE + 8, WIDTH),
            pltpu.SMEM((ROWS,), jnp.int32),
            pltpu.SMEM((DEPTH,), jnp.int32),
            pltpu.VMEM((WIDTH,), jnp.int32),
            pltpu.SemaphoreType.DMA((10,)),
        ],
        compiler_params=limit(4),
        name="pack_y",
    )(*[pltpu.with_memory_space_constraint(value, pltpu.MemorySpace.HBM) for value in arguments])
    slabs, subs = lax.axis_size("slab"), lax.axis_size("sub")
    down = [(s * subs + i + 1, s * subs + i) for s in range(1, slabs) for i in range(subs - 1)]
    up = [(j, i) for i, j in down]
    swaps = [[(i, i + 1) for i in range(start, subs - 1, 2)] for start in (0, 1)]
    swaps = [pairs + [(j, i) for i, j in pairs] for pairs in swaps]
    both = ("slab", "sub")
    y_parts = (
        lax.ppermute(first, both, down + swaps[0]), lax.ppermute(second, both, up + swaps[1])
    )
    chosen = pl.pallas_call(
        prepare,
        out_shape=jax.ShapeDtypeStruct((WIDTH, WIDTH), jnp.bfloat16),
        in_specs=[VMEM],
        out_specs=VMEM,
        compiler_params=limit(1),
        name="prepare",
    )(labels)
    first, second, y_below, y_above = pl.pallas_call(
        pack_z,
        out_shape=(f32(len(DOWN_PLANES), TALL, WIDTH),) * 2 + (f32(DOWN_SIZE + 8, WIDTH),) * 2,
        in_specs=[VMEM] * 6,
        out_specs=(VMEM,) * 4,
        compiler_params=limit(4),
        name="pack_z",
    )(labels, field_init, load, modulus, *y_parts)
    z_second = swap(second, "slab", 1)
    z_first = swap(first, "slab", 0)

    def sizes(planes):
        return [(3, planes, TALL, WIDTH)] * 2 + [(planes, TALL, WIDTH)] + [
            (n, planes, TALL, WIDTH) for n in (6, 12, 12)
        ]

    states = []
    for even in (False, True):
        states += pl.pallas_call(
            functools.partial(solve_inner, even),
            out_shape=[f32(*size) for size in sizes(DEPTH)] + [f32(3, 2, TALL, WIDTH)],
            in_specs=[VMEM] * 5,
            out_specs=[VMEM] * 7,
            compiler_params=limit(6),
        )(field_init, load, modulus, y_below, y_above)
    near = pl.pallas_call(
        solve_near,
        out_shape=(f32(3, 2, ROWS, WIDTH), f32(8, WIDTH)),
        in_specs=[VMEM] * 18,
        out_specs=(VMEM, VMEM),
        scratch_shapes=[scratch(8 * SY, WIDTH)] + [scratch(*size) for size in sizes(15)],
        compiler_params=limit(12),
        name="solve_near",
    )(labels, chosen, y_above, z_first, *states)
    return pl.pallas_call(
        solve_far,
        out_shape=(f32(3, DEPTH, ROWS, WIDTH), f32(6, SZ, SY * SX)),
        in_specs=[VMEM] * 20,
        out_specs=(hbm, VMEM),
        scratch_shapes=[scratch(8 * SY, WIDTH)] + [scratch(*size) for size in sizes(15)]
        + [pltpu.SemaphoreType.DMA((3,))],
        compiler_params=limit(14),
        name="solve_far",
    )(labels, chosen, y_above, z_second, *states, *near)


def solution(mesh):
    in_specs = (
        P(None, "slab", "sub", None),
        P(None, "slab", "sub", None),
        P("slab", "sub", None),
        P("slab"),
        P("sub"),
        P(),
    )
    out_specs = (P(None, "slab", "sub", None), P(None, "slab", "sub"))
    return jax.shard_map(
        on_device, mesh=mesh, in_specs=in_specs, out_specs=out_specs, check_vma=False
    )
```

```python
import functools

import jax
import jax.numpy as jnp
from jax import lax
from jax.experimental import pallas as pl
from jax.experimental.pallas import tpu as pltpu
from jax.sharding import PartitionSpec as P


SX = 32
SY = 4
SZ = 2
DEPTH = 8
ROWS = 16
WIDTH = 128
TALL = 24
DAMPING = 0.6

POISSON = 0.3
LAME = POISSON / ((1.0 + POISSON) * (1.0 - 2.0 * POISSON))
SHEAR = 0.5 / (1.0 + POISSON)

FIELD, LOAD, MODULUS = 0, 1, 2
UP_ROWS, DOWN_ROWS = (3, 2, 3), (4, 3, 3)
UP_AT, DOWN_AT = (0, 72, 120), (0, 96, 168)
DOWN_SIZE = 192
UP_PLANES = (
    [(FIELD, c, z) for c in range(3) for z in (5, 6, 7)]
    + [(LOAD, c, z) for c in range(3) for z in (6, 7)]
    + [(MODULUS, 0, z) for z in (5, 6, 7)]
)
DOWN_PLANES = (
    [(FIELD, c, z) for c in range(3) for z in (0, 1, 2, 3)]
    + [(LOAD, c, z) for c in range(3) for z in (0, 1, 2)]
    + [(MODULUS, 0, z) for z in (0, 1, 2)]
)


LABEL_PLANE = (MODULUS, 0, 0)


def y_rows(kind, c, z, up):
    rows, start = (UP_ROWS[kind], UP_AT[kind]) if up else (DOWN_ROWS[kind], DOWN_AT[kind])
    start += rows * (DEPTH * c + z)
    return slice(start, start + rows)


def is_even(axis):
    return lax.axis_index(axis) % 2 == 0


def pack_y(
    seg_y_hbm, seg_z_hbm, seg_x_hbm, field_hbm, load_hbm, modulus_hbm,
    first, second, field, load, modulus, labels, up, down, seg_y, seg_z, seg_x, sems,
):
    pairs = (
        (field_hbm, field), (load_hbm, load), (modulus_hbm, modulus),
        (seg_y_hbm, seg_y), (seg_z_hbm, seg_z), (seg_x_hbm, seg_x),
    )
    copies = [pltpu.make_async_copy(src, dst, sems.at[k]) for k, (src, dst) in enumerate(pairs)]
    for copy in copies:
        copy.start()
    for ref, kind in ((field, FIELD), (load, LOAD), (modulus, MODULUS)):
        copies[kind].wait()
        for c in range(1 if kind == MODULUS else 3):
            for z in range(DEPTH):
                at = (z,) if kind == MODULUS else (c, z)
                up[y_rows(kind, c, z, True), :] = ref[(*at, slice(ROWS - UP_ROWS[kind], ROWS), slice(None))]
                down[y_rows(kind, c, z, False), :] = ref[(*at, slice(0, DOWN_ROWS[kind]), slice(None))]
    for copy in copies[3:]:
        copy.wait()
    lane = lax.broadcasted_iota(jnp.int32, (DOWN_ROWS[MODULUS], WIDTH), 1)
    at = y_rows(*LABEL_PLANE, False)
    down[at, :] = jnp.where(lane == WIDTH - 1, seg_y[0].astype(jnp.float32), down[at, :])
    upward = (lax.axis_index("slab") == 0) & is_even("sub")
    first[...] = jnp.where(upward, up[...], down[...])
    second[...] = jnp.where(upward, down[...], up[...])
    for k in range(SY):
        labels[k : k + 1, :] = jnp.full((1, WIDTH), seg_y[4 * k].astype(jnp.float32))
    for k in range(SZ):
        labels[SY + k : SY + k + 1, :] = jnp.full((1, WIDTH), seg_z[4 * k].astype(jnp.float32))
    labels[7:8, :] = seg_x[...].reshape(1, WIDTH).astype(jnp.float32)


def edge_tile(below, above, kind, c, z):
    parts = [above[y_rows(kind, c, z, False), :]]
    spare = 8 - UP_ROWS[kind] - DOWN_ROWS[kind]
    parts.append(jnp.zeros((spare, WIDTH), jnp.float32))
    parts.append(below[y_rows(kind, c, z, True), :])
    return jnp.concatenate(parts, axis=0)


def pack_z(labels, field, load, modulus, y_first, y_second, first, second, y_below, y_above):
    below_first = (lax.axis_index("slab") == 0) & jnp.logical_not(is_even("sub"))
    y_below[...] = jnp.where(below_first, y_first[...], y_second[...])
    y_above[...] = jnp.where(below_first, y_second[...], y_first[...])
    even = is_even("slab")
    lane = lax.broadcasted_iota(jnp.int32, (TALL, WIDTH), 1)
    tall = {}

    def whole(kind, c, z):
        if (kind, c, z) not in tall:
            own = (field if kind == FIELD else load)[c, z] if kind != MODULUS else modulus[z]
            tall[kind, c, z] = jnp.concatenate(
                [own, edge_tile(y_below, y_above, kind, c, z)], axis=0
            )
        return tall[kind, c, z]

    for index, plane in enumerate(DOWN_PLANES):
        down = whole(*plane)
        if plane == LABEL_PLANE:
            down = jnp.where(lane == WIDTH - 1, labels[SY : SY + 1, :], down)
        up = whole(*UP_PLANES[index]) if index < len(UP_PLANES) else down
        first[index] = jnp.where(even, up, down)
        second[index] = jnp.where(even, down, up)


def roll_x(value, shift):
    return pltpu.roll(value, shift % WIDTH, 1)


def roll_y(value, shift):
    return pltpu.roll(value, shift % TALL, 0)


class Planes:
    def __init__(self, mine, offset, given=None):
        self.mine, self.offset, self.given = mine, offset, given
        self.written = set()

    def where(self, lead, z, tile, ref, offset):
        rows = slice(None) if tile is None else slice(8 * tile, 8 * tile + 8)
        return ref, (*lead, z + offset, rows, slice(None))

    def load(self, *lead, z, tile=None):
        own = {(*lead, z, t) in self.written for t in (range(3) if tile is None else (tile,))}
        assert len(own) == 1
        if own.pop():
            ref, at = self.where(lead, z, tile, self.mine, self.offset)
        else:
            ref, at = self.where(lead, z, tile, self.given, 0)
        return ref[at]

    def store(self, value, *lead, z, tile=None):
        self.written |= {(*lead, z, t) for t in (range(3) if tile is None else (tile,))}
        ref, at = self.where(lead, z, tile, self.mine, self.offset)
        ref[at] = value


def fill(state, planes, own_block=None, z_part=None):
    work, loads, elem = state[:3]
    slab_pos, sub_pos = lax.axis_index("slab"), lax.axis_index("sub")
    last_slab, last_sub = lax.axis_size("slab") - 1, lax.axis_size("sub") - 1

    def gather(kind, c, z):
        if z < 0:
            return z_part[UP_PLANES.index((kind, c, z + DEPTH))]
        if z >= DEPTH:
            return z_part[DOWN_PLANES.index((kind, c, z - DEPTH))]
        field, load, modulus, y_below, y_above = own_block
        own = (field if kind == FIELD else load)[c, z] if kind != MODULUS else modulus[z]
        return jnp.concatenate([own, edge_tile(y_below, y_above, kind, c, z)], axis=0)

    row = lax.broadcasted_iota(jnp.int32, (TALL, WIDTH), 0)
    lane = lax.broadcasted_iota(jnp.int32, (TALL, WIDTH), 1)
    inside = (lane < WIDTH - 1) & ((row != ROWS - 1) | (sub_pos != last_sub))
    inside_top = inside & (slab_pos != last_slab)
    for z in planes:
        if -3 <= z <= 10:
            value = gather(MODULUS, 0, z)
            elem.store(jnp.where(inside_top if z == DEPTH - 1 else inside, value, 0.0), z=z)
        for c in range(3):
            work.store(gather(FIELD, c, z), c, z=z)
            if -2 <= z <= 10:
                loads.store(gather(LOAD, c, z), c, z=z)


def invert(state, first, last):
    elem, inv = state[2], state[3]
    diag_scale = (LAME + 4.0 * SHEAR) / 9.0
    off_scale = (LAME + SHEAR) / 12.0
    before = None
    for z in range(first - 1, last + 1):
        e = elem.load(z=z)
        up = roll_y(e, 1)
        sum_y, dif_y = e + up, up - e
        sum_right, dif_right = roll_x(sum_y, 1), roll_x(dif_y, 1)
        now = (sum_y + sum_right, dif_y + dif_right, sum_right - sum_y, dif_right - dif_y)
        if before is not None:
            p = (diag_scale / off_scale) * (before[0] + now[0])
            cc = before[1] - now[1]
            b = before[2] - now[2]
            a = before[3] + now[3]
            pp = p * p
            co00, co11, co22 = pp - cc * cc, pp - b * b, pp - a * a
            co01, co02, co12 = b * cc - a * p, a * cc - b * p, a * b - p * cc
            det = p * co00 + a * co01 + b * co02
            scale = jnp.where(det != 0.0, (DAMPING / off_scale) / det, 0.0)
            for k, value in enumerate((co00, co01, co02, co11, co12, co22)):
                inv.store(value * scale, k, z=z)
        before = now


def spread(state, planes):
    work, modes = state[0], state[4]
    for c in range(3):
        for z in planes:
            v = work.load(c, z=z)
            up = roll_y(v, -1)
            sum_y, dif_y = v + up, up - v
            sum_left, dif_left = roll_x(sum_y, -1), roll_x(dif_y, -1)
            modes.store(sum_y + sum_left, 4 * c, z=z)
            modes.store(sum_left - sum_y, 4 * c + 1, z=z)
            modes.store(dif_y + dif_left, 4 * c + 2, z=z)
            modes.store(dif_left - dif_y, 4 * c + 3, z=z)


def stress(state, lo, hi, resume=False, join=False, low_end=True, high_end=True):
    elem, modes, forces = state[2], state[4], state[5]
    for tile in range(3):
        old = [modes.load(k, z=lo, tile=tile) for k in range(12)]
        held = [forces.load(k, z=lo, tile=tile) for k in range(12)] if resume else None
        for z in range(lo, hi):
            e = elem.load(z=z, tile=tile)
            new = [modes.load(k, z=z + 1, tile=tile) for k in range(12)]
            total = [None if k % 4 == 0 else new[k] + old[k] for k in range(12)]
            delta = [new[k] - old[k] for k in range(12)]
            xa, xb, xc = total[1], total[2], total[3]
            xd, xe, xf, xg = delta[0], delta[1], delta[2], delta[3]
            ya, yb, yc = total[5], total[6], total[7]
            yd, ye, yf, yg = delta[4], delta[5], delta[6], delta[7]
            za, zb, zc = total[9], total[10], total[11]
            zd, ze, zf, zg = delta[8], delta[9], delta[10], delta[11]
            lam0, mu0 = e * (LAME / 16.0), e * (SHEAR / 16.0)
            lam1, mu1 = e * (LAME / 48.0), e * (SHEAR / 48.0)
            twice = e * (SHEAR / 8.0)
            last_scale = e * ((LAME + 4.0 * SHEAR) / 144.0)
            t = lam0 * (xa + yb + zd)
            xy, xz, yz = mu0 * (xb + ya), mu0 * (xd + za), mu0 * (yd + zb)
            s_x, s_y, s_z = lam1 * (yc + ze), lam1 * (xc + zf), lam1 * (xe + yf)
            q = xf + ye + zc
            even = (
                None, t + twice * xa, xy, s_y + mu0 * xc,
                None, xy, t + twice * yb, s_x + mu0 * yc,
                None, xz, yz, mu1 * (q + zc),
            )
            odd = (
                xz, s_z + mu0 * xe, mu1 * (q + xf), last_scale * xg,
                yz, mu1 * (q + ye), s_z + mu0 * yf, last_scale * yg,
                t + twice * zd, s_x + mu0 * ze, s_y + mu0 * zf, last_scale * zg,
            )
            for k in range(12 if z > lo or low_end else 0):
                if even[k] is None:
                    low = -odd[k] if held is None else held[k] - odd[k]
                else:
                    low = even[k] - odd[k] if held is None else held[k] + (even[k] - odd[k])
                forces.store(low, k, z=z, tile=tile)
            if z < hi - 1 or high_end:
                held = [odd[k] if even[k] is None else even[k] + odd[k] for k in range(12)]
            old = new
        for k in range(12 if high_end else 0):
            total = forces.load(k, z=hi, tile=tile) + held[k] if join else held[k]
            forces.store(total, k, z=hi, tile=tile)


def misfit(state, z):
    loads, forces = state[1], state[5]
    out = []
    for c in range(3):
        f = [forces.load(4 * c + k, z=z) for k in range(4)]
        sum_y = (f[0] - f[1]) + roll_x(f[0] + f[1], 1)
        dif_y = (f[2] - f[3]) + roll_x(f[2] + f[3], 1)
        out.append(loads.load(c, z=z) - ((sum_y - dif_y) + roll_y(sum_y + dif_y, 1)))
    return out


def relax(state, planes):
    work, inv = state[0], state[3]
    table = ((0, 1, 2), (1, 3, 4), (2, 4, 5))
    for z in planes:
        m = [inv.load(k, z=z) for k in range(6)]
        r = misfit(state, z)
        for c in range(3):
            i, j, k = table[c]
            step = m[i] * r[0] + m[j] * r[1] + m[k] * r[2]
            work.store(work.load(c, z=z) + step, c, z=z)


def solve_inner(even, *refs):
    @pl.when(is_even("slab") == even)
    def mine():
        inner(*refs)


def inner(field, load, modulus, y_below, y_above, *refs):
    state = [Planes(ref, 0) for ref in refs[:6]]
    residual = refs[6]
    fill(state, range(0, 8), own_block=(field, load, modulus, y_below, y_above))
    invert(state, 1, 7)
    spread(state, range(0, 8))
    stress(state, 0, 7)
    relax(state, range(1, 7))
    spread(state, range(1, 7))
    stress(state, 1, 6)
    relax(state, range(2, 6))
    spread(state, range(2, 6))
    stress(state, 2, 5)
    for z in (3, 4):
        for c, value in enumerate(misfit(state, z)):
            residual[c, z - 3] = value


LOWER, UPPER = (0, 1), (6, 7)


def solve_side(lower, z_part, given, mine, smoothed):
    state = [Planes(ref, 3, old) for ref, old in zip(mine, given)]
    if lower:
        fill(state, range(-3, 0), z_part=z_part)
        invert(state, -2, 0)
        rounds = ((-3, 0), (-2, 1), (-1, 2))
    else:
        fill(state, range(8, 12), z_part=z_part)
        invert(state, 8, 10)
        rounds = ((7, 11), (6, 10), (5, 9))
    for step, (first, last) in enumerate(rounds):
        spread(state, range(first, last) if lower else range(first + 1, last + 1))
        stress(state, first, last, join=lower, resume=not lower, low_end=not lower, high_end=lower)
        if step < 2:
            relax(state, range(first + 1, last + 1) if lower else range(first, last))
        if step == 1:
            smoothed()
    return {z: misfit(state, z) for z in ((0, 1, 2) if lower else (5, 6, 7, 8))}


def prepare(labels, chosen):
    target = lax.broadcasted_iota(jnp.int32, (WIDTH, WIDTH), 0) % SX
    hit = jnp.where(target.astype(jnp.float32) == labels[7:8, :], 1.0, 0.0)
    chosen[...] = hit.astype(jnp.bfloat16)


def restrict(kz, residual, labels, chosen, y_label, z_label, rows):
    slab_pos, sub_pos = lax.axis_index("slab"), lax.axis_index("sub")
    last_slab, last_sub = lax.axis_size("slab") - 1, lax.axis_size("sub") - 1
    row = lax.broadcasted_iota(jnp.int32, (TALL, WIDTH), 0)

    def flag(value, segment):
        return jnp.where(value == segment.astype(jnp.float32), 1.0, 0.0)

    start_z = SZ * slab_pos + kz
    low = flag(labels[SY + kz : SY + kz + 1, :], start_z)
    if kz == 0:
        high = flag(labels[SY + 1 : SY + 2, :], start_z)
    else:
        high = jnp.where(slab_pos != last_slab, flag(z_label, start_z), 0.0)
    sums = [None] * 5
    for step in range(5):
        r = residual[4 * kz + step]
        if step in (0, 4):
            r = [(low if step == 0 else high) * value for value in r]
        q = 0.5 * (step - 2)
        terms = [r[0], r[1], r[2], q * r[1], q * r[0]]
        for k in range(5 if q != 0.0 else 3):
            sums[k] = terms[k] if sums[k] is None else sums[k] + terms[k]
    r0, r1, r2, z1, z0 = sums
    count_z, moment_z = low + 3.0 + high, high - low

    start_y = SY * sub_pos
    owns_next = jnp.where(sub_pos != last_sub, flag(y_label, start_y + SY - 1), 0.0)
    lane = lax.broadcasted_iota(jnp.int32, (1, WIDTH), 1)
    group = lane // SX
    seg_x = labels[7:8, :]
    q_x = 0.5 * (lane.astype(jnp.float32) - 4.0 * seg_x - 2.0)
    count_y = jnp.zeros((1, WIDTH), jnp.float32)
    moment_y = jnp.zeros((1, WIDTH), jnp.float32)

    def total(value):
        return jnp.sum(value, axis=0, keepdims=True)

    for ky in range(SY):
        first = flag(labels[ky : ky + 1, :], start_y + ky)
        final = flag(labels[ky + 1 : ky + 2, :], start_y + ky) if ky < SY - 1 else owns_next
        local = row - 4 * ky
        weight = jnp.where((local > 0) & (local < 4), 1.0, 0.0)
        weight = jnp.where(local == 0, first, jnp.where(local == 4, final, weight))
        moment = weight * (0.5 * (local - 2).astype(jnp.float32))
        count_y = jnp.where(group == ky, first + 3.0 + final, count_y)
        moment_y = jnp.where(group == ky, final - first, moment_y)
        plain = [total(weight * value) for value in (r0, r1, r2)]
        turned = [
            total(moment * r2 - weight * z1),
            total(weight * z0) - q_x * plain[2],
            q_x * plain[1] - total(moment * r0),
        ]
        for k, value in enumerate(plain + turned + [jnp.ones((1, WIDTH), jnp.float32), q_x]):
            rows[8 * ky + k : 8 * ky + k + 1, :] = value

    rest, parts = rows[...], []
    for _ in range(3):
        parts.append(rest.astype(jnp.bfloat16))
        rest = rest - parts[-1].astype(jnp.float32)
    totals = lax.dot_general(
        jnp.concatenate(parts, axis=0), chosen[...], (((1,), (1,)), ((), ())),
        preferred_element_type=jnp.float32,
    )
    totals = totals[0:32] + totals[32:64] + totals[64:96]
    s = totals[0:8]
    for ky in range(1, SY):
        s = jnp.where(group == ky, totals[8 * ky : 8 * ky + 8], s)
    s = [s[k : k + 1] for k in range(8)]
    count_x, moment_x = s[6], s[7]
    count = count_x * count_y * count_z
    centre = [
        moment_x * count_y * count_z / count,
        count_x * moment_y * count_z / count,
        count_x * count_y * moment_z / count,
    ]
    scale = 1.0 / jnp.sqrt(count)
    turned = [
        s[3] - (centre[1] * s[2] - centre[2] * s[1]),
        s[4] - (centre[2] * s[0] - centre[0] * s[2]),
        s[5] - (centre[0] * s[1] - centre[1] * s[0]),
    ]
    return [value * scale for value in s[:3] + turned]


def last_lane(row):
    return jnp.broadcast_to(row[:, WIDTH - 1 :], (1, WIDTH))


def z_label(part):
    return last_lane(part[DOWN_PLANES.index(LABEL_PLANE), 0:1, :])


def with_middle(residual, middle):
    residual |= {z: [middle[c, z - 3] for c in range(3)] for z in (3, 4)}
    return residual


def solve_near(labels, chosen, y_above, z_first, *refs):
    states, (smooth, coarse), rows, mine = (refs[7:14], refs[:7]), refs[14:16], refs[16], refs[17:23]
    for lower in (False, True):
        *given, middle = states[lower]

        @pl.when(is_even("slab") != lower)
        def side(given=given, middle=middle):
            def smoothed():
                for k, z in enumerate(LOWER if lower else UPPER):
                    for c in range(3):
                        smooth[c, k] = mine[0][c, z + 3, :ROWS, :]

            residual = solve_side(lower, z_first, given, mine, smoothed)
            coarse_rows = restrict(
                0 if lower else 1, with_middle(residual, middle), labels, chosen,
                last_lane(y_above[DOWN_AT[MODULUS] : DOWN_AT[MODULUS] + 1, :]), z_label(z_first), rows,
            )
            for k in range(6):
                coarse[k : k + 1, :] = coarse_rows[k]


def solve_far(labels, chosen, y_above, z_second, *refs):
    states, (near_smooth, near_coarse) = (refs[:7], refs[7:14]), refs[14:16]
    (smooth, coarse), rows, mine, sems = refs[16:18], refs[18], refs[19:25], refs[25]

    for lower in (True, False):
        *given, middle = states[lower]

        @pl.when(is_even("slab") == lower)
        def side(given=given, middle=middle):
            near, far, kz = (UPPER, LOWER, 0) if lower else (LOWER, UPPER, 1)
            planes = slice(far[0] + 3, far[1] + 4)
            copies = [
                pltpu.make_async_copy(src, smooth.at[:, out], sems.at[k])
                for k, (src, out) in enumerate((
                    (given[0].at[:, 2:6, :ROWS, :], slice(2, 6)),
                    (near_smooth, slice(near[0], near[1] + 1)),
                    (mine[0].at[:, planes, :ROWS, :], slice(far[0], far[1] + 1)),
                ))
            ]
            copies[0].start()
            copies[1].start()
            residual = solve_side(lower, z_second, given, mine, copies[2].start)
            coarse_rows = restrict(
                kz, with_middle(residual, middle), labels, chosen,
                last_lane(y_above[DOWN_AT[MODULUS] : DOWN_AT[MODULUS] + 1, :]), z_label(z_second), rows,
            )
            for k in range(6):
                coarse[k, kz : kz + 1, :] = coarse_rows[k]
                coarse[k, 1 - kz : 2 - kz, :] = near_coarse[k : k + 1, :]
            for copy in copies:
                copy.wait()


VMEM = pl.BlockSpec(memory_space=pltpu.VMEM)


def f32(*shape):
    return jax.ShapeDtypeStruct(shape, jnp.float32)


def scratch(*shape):
    return pltpu.VMEM(shape, jnp.float32)


def on_device(field_init, load, modulus, seg_z, seg_y, seg_x):
    def swap(block, axis, start):
        pairs = [(i, i + 1) for i in range(start, lax.axis_size(axis) - 1, 2)]
        return lax.ppermute(block, axis, pairs + [(j, i) for i, j in pairs])

    def limit(mib):
        return pltpu.CompilerParams(vmem_limit_bytes=mib << 20)

    hbm = pl.BlockSpec(memory_space=pltpu.MemorySpace.HBM)
    blocks = [f32(3, DEPTH, ROWS, WIDTH), f32(3, DEPTH, ROWS, WIDTH), f32(DEPTH, ROWS, WIDTH)]
    arguments = (seg_y, seg_z, seg_x, field_init, load, modulus)
    first, second, field_init, load, modulus, labels = pl.pallas_call(
        pack_y,
        out_shape=[f32(DOWN_SIZE, WIDTH), f32(DOWN_SIZE, WIDTH)] + blocks + [f32(8, WIDTH)],
        in_specs=[hbm] * 6,
        out_specs=[VMEM] * 6,
        scratch_shapes=[
            scratch(DOWN_SIZE, WIDTH),
            scratch(DOWN_SIZE, WIDTH),
            pltpu.SMEM((ROWS,), jnp.int32),
            pltpu.SMEM((DEPTH,), jnp.int32),
            pltpu.VMEM((WIDTH,), jnp.int32),
            pltpu.SemaphoreType.DMA((6,)),
        ],
        compiler_params=limit(4),
        name="pack_y",
    )(*[pltpu.with_memory_space_constraint(value, pltpu.MemorySpace.HBM) for value in arguments])
    slabs, subs = lax.axis_size("slab"), lax.axis_size("sub")
    down = [(s * subs + i + 1, s * subs + i) for s in range(1, slabs) for i in range(subs - 1)]
    up = [(j, i) for i, j in down]
    swaps = [[(i, i + 1) for i in range(start, subs - 1, 2)] for start in (0, 1)]
    swaps = [pairs + [(j, i) for i, j in pairs] for pairs in swaps]
    both = ("slab", "sub")
    y_parts = (
        lax.ppermute(first, both, down + swaps[0]), lax.ppermute(second, both, up + swaps[1])
    )
    chosen = pl.pallas_call(
        prepare,
        out_shape=jax.ShapeDtypeStruct((WIDTH, WIDTH), jnp.bfloat16),
        in_specs=[VMEM],
        out_specs=VMEM,
        compiler_params=limit(1),
        name="prepare",
    )(labels)
    first, second, y_below, y_above = pl.pallas_call(
        pack_z,
        out_shape=(f32(len(DOWN_PLANES), TALL, WIDTH),) * 2 + (f32(DOWN_SIZE, WIDTH),) * 2,
        in_specs=[VMEM] * 6,
        out_specs=(VMEM,) * 4,
        compiler_params=limit(4),
        name="pack_z",
    )(labels, field_init, load, modulus, *y_parts)
    z_second = swap(second, "slab", 1)
    z_first = swap(first, "slab", 0)

    def sizes(planes):
        return [(3, planes, TALL, WIDTH)] * 2 + [(planes, TALL, WIDTH)] + [
            (n, planes, TALL, WIDTH) for n in (6, 12, 12)
        ]

    states = []
    for even in (False, True):
        states += pl.pallas_call(
            functools.partial(solve_inner, even),
            out_shape=[f32(*size) for size in sizes(DEPTH)] + [f32(3, 2, TALL, WIDTH)],
            in_specs=[VMEM] * 5,
            out_specs=[VMEM] * 7,
            compiler_params=limit(6),
        )(field_init, load, modulus, y_below, y_above)
    near = pl.pallas_call(
        solve_near,
        out_shape=(f32(3, 2, ROWS, WIDTH), f32(8, WIDTH)),
        in_specs=[VMEM] * 18,
        out_specs=(VMEM, VMEM),
        scratch_shapes=[scratch(8 * SY, WIDTH)] + [scratch(*size) for size in sizes(15)],
        compiler_params=limit(12),
        name="solve_near",
    )(labels, chosen, y_above, z_first, *states)
    return pl.pallas_call(
        solve_far,
        out_shape=(f32(3, DEPTH, ROWS, WIDTH), f32(6, SZ, SY * SX)),
        in_specs=[VMEM] * 20,
        out_specs=(hbm, VMEM),
        scratch_shapes=[scratch(8 * SY, WIDTH)] + [scratch(*size) for size in sizes(15)]
        + [pltpu.SemaphoreType.DMA((3,))],
        compiler_params=limit(14),
        name="solve_far",
    )(labels, chosen, y_above, z_second, *states, *near)


def solution(mesh):
    in_specs = (
        P(None, "slab", "sub", None),
        P(None, "slab", "sub", None),
        P("slab", "sub", None),
        P("slab"),
        P("sub"),
        P(),
    )
    out_specs = (P(None, "slab", "sub", None), P(None, "slab", "sub"))
    return jax.shard_map(
        on_device, mesh=mesh, in_specs=in_specs, out_specs=out_specs, check_vma=False
    )
```
